32 devices in a mesh: region: 8 (over z, y), lev: 4 (over x, core).
Axes of the slice: x: 2, y: 2, z: 4, core: 2. Of those that a mesh axis runs over, the one named last changes fastest.
Arguments:
- background_members: bfloat16 [80, 16, 1024, 8], P(None, 'lev', 'region'), may hold values from -6 to 6
- channel_height_kernel: float32 [8, 16], P(None, 'lev'), may hold values from -1.5 to 1.5
- sensor_spread_down: float32 [4], replicated, may hold values from 0.2 to 0.6
- sensor_spread_across: float32 [4], replicated, may hold values from 0.2 to 0.6
- measurement_placement: int32 [4, 64], replicated, may hold values from 0 to 511
- measurement_ordering: int32 [4, 64], replicated, may hold values from 0 to 63, each once within a row
- group_area_number: int32 [4], replicated, may hold values from 0 to 7
- taper_radius_limit: int32 [8], replicated, may hold values from 8 to 16
- measured_amounts: float32 [4, 64], replicated, may hold values from -8 to 8
- measurement_noise_spread: float32 [4, 64], replicated, may hold values from 0.05 to 0.5
Outputs:
- analysis: bfloat16 [80, 16, 8, 1024], P(None, 'lev', 'region')
The draws below stay inside these ranges and needn't reach their ends.
All inputs are finite; a program needn't handle non-finite values.
Results may differ from the reference program's by a relative error of at most 0.001.
Values may be sent and summed in bfloat16 or wider, within the bound.
No kernel may reach another device: no remote copies, remote signals or barrier semaphores. Data moves between devices by JAX's collectives and lax.ppermute only.
A program may use at most 128 MiB of HBM per device.

```python
import math
import jax
import jax.numpy as jnp
from jax import lax

MEMBER_COUNT = 80
TILE = 32
STRIDE = 4
CHAN = 8
BATCH = 64
NBATCH = 4
HEIGHT_LAYERS = 16
AREA_CELLS = 1024
SITES = 512
RADIUS = 16
N_REGION = 8


def touch_ends(values, stream_key, low, high):
    longest = values.shape.index(max(values.shape))
    spots = []
    for shift in (0, 1):
        where = [jax.random.randint(jax.random.fold_in(stream_key, axis), (), 0, length) for axis, length in enumerate(values.shape)]
        where[longest] = (where[longest] + shift) % values.shape[longest]
        spots.append(tuple(where))
    return values.at[spots[0]].set(low).at[spots[1]].set(high)


def block_scale(own_key, dims, split, least, largest):
    level = 1.0
    for dim, shards_of in split:
        steps = jax.random.uniform(jax.random.fold_in(jax.random.fold_in(own_key, 6), dim), (shards_of,), jnp.float32, least / len(split), largest / len(split))
        level = level * jnp.repeat(jnp.exp(steps), dims[dim] // shards_of).reshape((-1,) + (1,) * (len(dims) - 1 - dim))
    return level


def gaussian(rng, extent, scale, bound, cuts=(), kind=jnp.bfloat16):
    gain = block_scale(rng, extent, cuts, -0.22, 0.18) if cuts else 1.0
    values = jax.random.normal(rng, extent, jnp.float32) * scale * gain
    return jnp.minimum(jnp.maximum(values, -bound), bound).astype(kind)


def setup_inputs(seed: int = 0) -> dict:
    seeds = jax.random.split(jax.random.key(seed), 11)
    background_members = gaussian(seeds[0], (MEMBER_COUNT, HEIGHT_LAYERS, AREA_CELLS, N_REGION), 1.0, 6.0, ((1, 4), (2, 8)))
    channel_height_kernel = gaussian(seeds[1], (CHAN, HEIGHT_LAYERS), HEIGHT_LAYERS ** -0.5, 1.5, ((1, 4),), jnp.float32)
    sensor_spread_down = jnp.clip(jax.random.uniform(seeds[2], (STRIDE,), jnp.float32, 0.2, 0.6), 0.2, 0.6)
    sensor_spread_across = jnp.clip(jax.random.uniform(seeds[3], (STRIDE,), jnp.float32, 0.2, 0.6), 0.2, 0.6)
    measurement_placement = touch_ends(jax.random.randint(seeds[4], (NBATCH, BATCH), 0, SITES), jax.random.fold_in(seeds[4], 1), 0, SITES - 1).astype(jnp.int32)
    measurement_ordering = jax.vmap(lambda own: jax.random.permutation(own, BATCH))(jax.random.split(seeds[5], NBATCH)).reshape((NBATCH, BATCH)).astype(jnp.int32)
    group_area_number = touch_ends(jax.random.randint(seeds[6], (NBATCH,), 0, N_REGION), jax.random.fold_in(seeds[6], 1), 0, N_REGION - 1).astype(jnp.int32)
    taper_radius_limit = touch_ends(jax.random.randint(seeds[7], (CHAN,), N_REGION, RADIUS + 1), jax.random.fold_in(seeds[7], 1), N_REGION, RADIUS).astype(jnp.int32)
    measured_amounts = gaussian(seeds[8], (NBATCH, BATCH), 1.5, 8.0, (), jnp.float32)
    measurement_noise_spread = jnp.clip(jnp.exp(jax.random.uniform(seeds[9], (NBATCH, BATCH), jnp.float32, math.log(0.05), math.log(0.5))), 0.05, 0.5)
    return {"background_members": background_members, "channel_height_kernel": channel_height_kernel, "sensor_spread_down": sensor_spread_down, "sensor_spread_across": sensor_spread_across, "measurement_placement": measurement_placement, "measurement_ordering": measurement_ordering, "group_area_number": group_area_number, "taper_radius_limit": taper_radius_limit, "measured_amounts": measured_amounts, "measurement_noise_spread": measurement_noise_spread}


highest = lax.Precision.HIGHEST

def footprint(present_state_grid, sensor_spread_down, sensor_spread_across, channel_height_kernel):
    members, levels, pixels = present_state_grid.shape
    foot_cells = TILE // STRIDE
    tiles_view = present_state_grid.reshape(members, levels, foot_cells, STRIDE, foot_cells, STRIDE)
    blocks = jnp.einsum('klaicj,i,j->klac', tiles_view, sensor_spread_down, sensor_spread_across, precision=highest)
    blocks = blocks.reshape(members, levels, foot_cells * foot_cells)
    weighted = jnp.einsum('klq,hl->khq', blocks, channel_height_kernel, precision=highest)
    return weighted.reshape(members, -1)

def taper_weight(distance, cut_radius):
    return jnp.maximum(0.0, 1.0 - distance / (cut_radius + 1.0))

def reference(background_members, channel_height_kernel, sensor_spread_down, sensor_spread_across, measurement_placement, measurement_ordering, group_area_number, taper_radius_limit, measured_amounts, measurement_noise_spread):
    denominator = MEMBER_COUNT - 1.0
    foot_cells = TILE // STRIDE * (TILE // STRIDE)
    places = jnp.arange(N_REGION).astype(jnp.float32)
    subdomain_state_grid = jnp.transpose(background_members, (3, 0, 1, 2))
    transforms = jnp.tile(jnp.eye(MEMBER_COUNT, dtype=jnp.float32)[None], (N_REGION, 1, 1))
    offsets = jnp.zeros((N_REGION, MEMBER_COUNT), jnp.float32)
    for batch_id in range(NBATCH):
        home_region = group_area_number[batch_id]
        start_members = subdomain_state_grid[home_region].astype(jnp.float32)
        priors = footprint(start_members, sensor_spread_down, sensor_spread_across, channel_height_kernel)
        picked = jnp.take(measurement_placement[batch_id], measurement_ordering[batch_id]).astype(jnp.int32)
        base_priors = jnp.take(priors, picked, axis=1)
        values = jnp.take(measured_amounts[batch_id], measurement_ordering[batch_id])
        errors = jnp.take(measurement_noise_spread[batch_id], measurement_ordering[batch_id])
        channels = picked // foot_cells
        cut_radius = jnp.take(taper_radius_limit, channels).astype(jnp.float32)
        center = lax.optimization_barrier(jnp.mean(base_priors, axis=0))
        anomaly = base_priors - center[None]
        current = jnp.dot(transforms[home_region].T, anomaly, precision=highest) + (center + jnp.dot(offsets[home_region], anomaly, precision=highest))[None]
        spacing = jnp.abs(places - home_region.astype(jnp.float32))

        def assimilate(state_carry, inputs):
            current, transforms, offsets = state_carry
            index_obs, value_obs, error_obs, cut_obs = inputs
            column = lax.dynamic_index_in_dim(current, index_obs, 1, keepdims=False)
            center_col = jnp.mean(column)
            anomaly_col = column - center_col
            variance = jnp.sum(anomaly_col * anomaly_col) / denominator + error_obs
            alpha_gain = 1.0 / (1.0 + jnp.sqrt(error_obs / variance))
            innovation = value_obs - center_col
            anomaly_all = current - lax.optimization_barrier(jnp.mean(current, axis=0, keepdims=True))
            covariance = jnp.dot(anomaly_col, anomaly_all, precision=highest) / denominator
            current = current + jnp.outer(innovation - alpha_gain * anomaly_col, covariance / variance)
            tapers = taper_weight(spacing, cut_obs)
            mapped = jnp.einsum('rkm,m->rk', transforms, anomaly_col, precision=highest)
            offsets = offsets + (tapers * innovation / (denominator * variance))[:, None] * mapped
            transforms = transforms - (tapers * alpha_gain / (denominator * variance))[:, None, None] * mapped[:, :, None] * anomaly_col[None, None, :]
            return ((current, transforms, offsets), None)
        indices = jnp.arange(BATCH, dtype=jnp.int32)
        final_carry, unused = lax.scan(assimilate, (current, transforms, offsets), (indices, values, errors, cut_radius))
        transforms, offsets = (final_carry[1], final_carry[2])

    def finish(inputs):
        start_members, transform_reg, offset_reg = inputs
        field_reg = start_members.astype(jnp.float32).reshape(MEMBER_COUNT, -1)
        center_reg = lax.optimization_barrier(jnp.mean(field_reg, axis=0))
        anomaly_reg = field_reg - center_reg[None]
        mixing = transform_reg + offset_reg[:, None]
        result = jnp.dot(mixing.T, anomaly_reg, precision=highest) + center_reg[None]
        return result.astype(jnp.bfloat16).reshape(MEMBER_COUNT, HEIGHT_LAYERS, TILE * TILE)
    stacked = lax.map(finish, (subdomain_state_grid, transforms, offsets))
    return jnp.transpose(stacked, (1, 2, 0, 3))
```

```python
import functools

import jax
import jax.numpy as jnp
from jax import lax
from jax.experimental import pallas as pl
from jax.experimental.pallas import tpu as pltpu
from jax.sharding import PartitionSpec as P

TILE = 32
STRIDE = 4
LANES = 128
SUB = 8

highest = lax.Precision.HIGHEST
f32 = jnp.float32
bf16 = jnp.bfloat16


def dot(a, b, ca, cb, precision=highest):
    return lax.dot_general(
        a, b, (((ca,), (cb,)), ((), ())), precision=precision, preferred_element_type=f32
    )


def iota(shape, dim):
    return lax.broadcasted_iota(jnp.int32, shape, dim)


def split3(x):
    hi = x.astype(bf16)
    rest = x - hi.astype(f32)
    mid = rest.astype(bf16)
    low = (rest - mid.astype(f32)).astype(bf16)
    return hi, mid, low


def prior_kernel(
    first_ref, down_ref, across_ref, home_ref, state_ref, kernel_ref, order_ref, table_ref,
    prior_ref, aux_ref,
):
    members, levels, regions, pixels = state_ref.shape
    count = order_ref.shape[1]
    batches = home_ref.shape[0]
    size = count // batches
    channels = kernel_ref.shape[0]
    sites = (TILE // STRIDE) * (TILE // STRIDE)

    lane = iota((1, count), 1)
    spread = jnp.where(
        iota((batches, count), 1) // size == iota((batches, count), 0), 1.0, 0.0
    ).astype(f32)
    hit = order_ref[...] == iota((size, count), 0)
    rows = []
    for name in range(3):
        wide = dot(table_ref[name], spread, 0, 0)
        rows.append(jnp.sum(jnp.where(hit, wide, 0.0), axis=0, keepdims=True))
    aux_ref[...] = jnp.concatenate(rows + [jnp.zeros((SUB - 3, count), f32)], axis=0)

    picked = rows[0].astype(jnp.int32)
    channel = picked // sites
    spot = picked - channel * sites
    spot_row = spot // (TILE // STRIDE)
    spot_col = spot - spot_row * (TILE // STRIDE)

    pixel = iota((pixels, 1), 0) + first_ref[0]
    row = pixel // TILE
    col = pixel - row * TILE
    weight_row = jnp.zeros((pixels, 1), f32)
    weight_col = jnp.zeros((pixels, 1), f32)
    for i in range(STRIDE):
        weight_row = jnp.where(row % STRIDE == i, down_ref[i], weight_row)
        weight_col = jnp.where(col % STRIDE == i, across_ref[i], weight_col)
    weight = weight_row * weight_col
    inside = (row // STRIDE == spot_row) & (col // STRIDE == spot_col)
    place = jnp.where(inside, weight, 0.0)

    total = jnp.zeros((members * regions, count), f32)
    for level in range(levels):
        height = jnp.zeros((1, count), f32)
        for c in range(channels):
            height = jnp.where(channel == c, kernel_ref[c, level], height)
        grid = state_ref[:, level].astype(f32).reshape(members * regions, pixels).astype(bf16)
        for piece in split3(place * height):
            total = total + dot(grid, piece, 1, 0, None)
    home = jnp.zeros((1, count), jnp.int32)
    for k in range(batches):
        home = jnp.where(lane // size == k, home_ref[k], home)
    here = iota((regions, count), 0) == home
    chosen = jnp.where(here[None], total.reshape(members, regions, count), 0.0)
    prior_ref[:members] = jnp.sum(chosen, axis=1)
    if prior_ref.shape[0] > members:
        prior_ref[members:] = jnp.zeros((prior_ref.shape[0] - members, count), f32)


def rep(x):
    return jnp.broadcast_to(x, (SUB, x.shape[1]))


def col(x, j):
    return jnp.broadcast_to(x[:, j : j + 1], (SUB, LANES))


def filter_kernel(members, own_ref, home_ref, radius_ref, base_ref, aux_ref, high_ref, low_ref, x_ref, h_ref, b_ref):
    padded, count = base_ref.shape
    batches = home_ref.shape[0]
    size = count // batches
    groups = size // SUB
    channels = radius_ref.shape[0]
    sites = (TILE // STRIDE) * (TILE // STRIDE)
    dof = members - 1.0
    E = padded
    lane = iota((1, LANES), 1)
    member = lane < members

    base = base_ref[...]
    if padded < LANES:
        base = jnp.concatenate([base, jnp.zeros((LANES - padded, count), f32)], axis=0)
    cols = base.T
    aux = aux_ref[...]
    aux_cols = jnp.concatenate([aux, jnp.zeros((LANES - SUB, count), f32)], axis=0).T
    center = jnp.sum(jnp.where(member, cols, 0.0), axis=1, keepdims=True) / members
    x_ref[:count] = jnp.where(
        lane == E, center - aux_cols[:, 1:2], jnp.where(member, cols - center, 0.0)
    )
    square = iota((LANES, LANES), 0)
    x_ref[count:] = jnp.where((square == iota((LANES, LANES), 1)) & (square < members), 1.0, 0.0)

    place = aux_cols[:, 0:1].astype(jnp.int32) // sites
    cut = jnp.zeros((count, 1), f32)
    for c in range(channels):
        cut = jnp.where(place == c, radius_ref[c].astype(f32), cut)
    inverse_cut = 1.0 / (cut + 1.0)
    noise = aux_cols[:, 2:3] * dof

    wide = count + LANES
    owner = jnp.zeros((1, wide), jnp.int32) + own_ref[0]
    for k in range(batches):
        owner = jnp.where(iota((1, wide), 1) // size == k, home_ref[k], owner)

    for b in range(batches):
        r0 = b * size
        xb = x_ref[r0 : r0 + size]
        xm = jnp.where(member, xb, 0.0)
        gram = dot(xm, xm, 1, 1)
        noise_b = noise[r0 : r0 + size]
        gram = gram + jnp.where(iota((size, size), 0) == iota((size, size), 1), noise_b, 0.0)
        G = [gram[SUB * g : SUB * g + SUB] for g in range(groups)]
        X = [xb[SUB * g : SUB * g + SUB] for g in range(groups)]
        for p in range(groups):
            C = [[col(G[g], SUB * p + j) for g in range(p, groups)] for j in range(SUB)]
            s = [[rep(C[j][0][i : i + 1]) for j in range(i + 1)] for i in range(SUB)]
            noise_p = jnp.broadcast_to(noise_b[SUB * p : SUB * p + SUB], (SUB, LANES))
            l = [[None] * SUB for _ in range(SUB)]
            inv = []
            for j in range(SUB):
                inv.append(1.0 / s[j][j])
                for i in range(j + 1, SUB):
                    l[i][j] = s[i][j] * inv[j]
                for i in range(j + 1, SUB):
                    for k in range(j + 1, i + 1):
                        s[i][k] = s[i][k] - l[i][j] * s[k][j]
            U, H, alpha = [], [], []
            for j in range(SUB):
                inv_alpha = 1.0 + jnp.sqrt(rep(noise_p[j : j + 1]) * inv[j])
                alpha.append(1.0 / inv_alpha)
                u = rep(G[p][j : j + 1])
                h = rep(X[p][j : j + 1])
                for i in range(j):
                    u = u - l[j][i][:, :size] * U[i]
                    h = h - (l[j][i] * alpha[i]) * H[i]
                h = jnp.where(lane == E, h * inv_alpha, h)
                U.append(u)
                H.append(h)
                row = jnp.where(lane == E + 1, alpha[j] * inv[j], h)
                h_ref[SUB * p + j : SUB * p + j + 1] = row[:1]
            for g in range(p + 1, groups):
                L = []
                for j in range(SUB):
                    c = C[j][g - p]
                    for i in range(j):
                        c = c - L[i] * s[j][i]
                    L.append(c * inv[j])
                for j in range(SUB):
                    G[g] = G[g] - L[j][:, :size] * U[j]
                    X[g] = X[g] - (L[j] * alpha[j]) * H[j]

        low = min((r0 + size) // LANES * LANES, count)
        span = wide - low
        hb = h_ref[...]
        hm = jnp.where(member, hb, 0.0)
        overlap = dot(hm, hm, 1, 1)
        xr = x_ref[low:]
        W = dot(hm, xr, 1, 1)
        far = jnp.abs(owner[:, low:] - home_ref[b]).astype(f32)
        taper = jnp.maximum(0.0, 1.0 - far * inverse_cut[r0 : r0 + size]) * hb[:, E + 1 : E + 2]
        S = [overlap[SUB * g : SUB * g + SUB] for g in range(groups)]
        W = [W[SUB * g : SUB * g + SUB] for g in range(groups)]
        tiles = span // LANES

        def scale(c, row):
            return jnp.concatenate(
                [c * row[:, LANES * t : LANES * t + LANES] for t in range(tiles)], axis=1
            )

        for p in range(groups):
            C = [[col(S[g], SUB * p + j) for g in range(p, groups)] for j in range(SUB)]
            B = []
            for j in range(SUB):
                w = rep(W[p][j : j + 1])
                for i in range(j):
                    w = w - scale(rep(C[i][0][j : j + 1]), B[i])
                beta = w * rep(taper[SUB * p + j : SUB * p + j + 1])
                B.append(beta)
                b_ref[SUB * p + j : SUB * p + j + 1, low:] = beta[:1]
            for g in range(p + 1, groups):
                for j in range(SUB):
                    W[g] = W[g] - scale(C[j][g - p], B[j])
        x_ref[low:] = xr - dot(b_ref[:, low:], hb, 0, 0)

    last = x_ref[count : count + members]
    mixing = jnp.where(member, last + last[:, E : E + 1], 0.0)
    mixing = mixing - jnp.sum(mixing, axis=0, keepdims=True) / members + 1.0 / members
    high = mixing.astype(bf16)
    high_ref[...] = high
    low_ref[...] = (mixing - high.astype(f32)).astype(bf16)


def swap(x, axis, n, k):
    return lax.ppermute(x, axis, [(i, i ^ k) for i in range(n)])


def reduce_over(x, axis, n):
    if n & (n - 1):
        return lax.psum(x, axis)
    stride = 1
    while stride < n:
        radix = 2 if (n // stride).bit_length() % 2 == 0 else 4
        x = x + sum(swap(x, axis, n, k * stride) for k in range(1, radix))
        stride *= radix
    return x


def total_over(x, region_count, level_count):
    rows, count = x.shape
    if level_count & (level_count - 1):
        return lax.psum(x, ("region", "lev"))
    me = lax.axis_index("lev")
    parts = x.reshape(level_count, rows // level_count, count)
    own = lax.dynamic_index_in_dim(parts, me, 0, keepdims=False)
    for k in range(1, level_count):
        piece = lax.dynamic_index_in_dim(parts, me ^ k, 0, keepdims=False)
        own = own + swap(piece, "lev", level_count, k)
    own = reduce_over(own, "region", region_count)
    held = jnp.stack([own] + [swap(own, "lev", level_count, k) for k in range(1, level_count)])
    return jnp.concatenate(
        [lax.dynamic_index_in_dim(held, me ^ v, 0, keepdims=False) for v in range(level_count)]
    )


def body(
    region_count,
    level_count,
    background_members,
    channel_height_kernel,
    sensor_spread_down,
    sensor_spread_across,
    measurement_placement,
    measurement_ordering,
    group_area_number,
    taper_radius_limit,
    measured_amounts,
    measurement_noise_spread,
):
    members, levels, pixels, regions = background_members.shape
    batches, size = measurement_ordering.shape
    count = batches * size
    own_region = lax.axis_index("region").astype(jnp.int32)

    state = jnp.transpose(background_members, (0, 1, 3, 2))
    if regions > 8:
        local = jnp.take(state, group_area_number, axis=2)
        home = jnp.arange(batches, dtype=jnp.int32)
    else:
        local, home = state, group_area_number
    table = jnp.stack(
        [measurement_placement.astype(f32), measured_amounts, measurement_noise_spread]
    )
    granule = SUB * level_count
    padded = -(-members // granule) * granule
    vmem = pl.BlockSpec(memory_space=pltpu.VMEM)
    smem = pl.BlockSpec(memory_space=pltpu.SMEM)
    partial, aux = pl.pallas_call(
        prior_kernel,
        out_shape=(
            jax.ShapeDtypeStruct((padded, count), f32),
            jax.ShapeDtypeStruct((SUB, count), f32),
        ),
        in_specs=[smem, smem, smem, smem, vmem, smem, vmem, vmem],
        out_specs=(vmem, vmem),
    )(
        (own_region * pixels)[None],
        sensor_spread_down,
        sensor_spread_across,
        home,
        local,
        channel_height_kernel,
        measurement_ordering.reshape(1, count),
        table,
    )
    base = total_over(partial, region_count, level_count)
    base, state = lax.optimization_barrier((base, state))
    pieces = pl.pallas_call(
        functools.partial(filter_kernel, members),
        out_shape=[jax.ShapeDtypeStruct((members, LANES), bf16)] * 2,
        in_specs=[smem, smem, smem, vmem, vmem],
        out_specs=[vmem, vmem],
        scratch_shapes=[
            pltpu.VMEM((count + LANES, LANES), f32),
            pltpu.VMEM((size, LANES), f32),
            pltpu.VMEM((size, count + LANES), f32),
        ],
        cost_estimate=pl.CostEstimate(flops=10**9, bytes_accessed=10**6, transcendentals=0),
    )(own_region[None], group_area_number, taper_radius_limit, base, aux)

    whole = lax.all_to_all(
        jnp.transpose(state, (2, 1, 0, 3)), "region", split_axis=0, concat_axis=0, tiled=True
    )
    field = jnp.transpose(whole, (2, 1, 0, 3)).reshape(members, -1)
    result = sum(dot(piece[:, :members], field, 0, 0, None) for piece in pieces)
    return result.reshape(members, levels, 1, pixels * region_count).astype(bf16)


def solution(mesh):
    return jax.shard_map(
        functools.partial(body, mesh.shape["region"], mesh.shape["lev"]),
        mesh=mesh,
        in_specs=(
            P(None, "lev", "region", None),
            P(None, "lev"),
            P(),
            P(),
            P(),
            P(),
            P(),
            P(),
            P(),
            P(),
        ),
        out_specs=P(None, "lev", "region", None),
        check_vma=False,
    )
```

```python
import functools

import jax
import jax.numpy as jnp
from jax import lax
from jax.experimental import pallas as pl
from jax.experimental.pallas import tpu as pltpu
from jax.sharding import PartitionSpec as P


TILE = 32
STRIDE = 4
LANES = 128
SUB = 8

highest = lax.Precision.HIGHEST
f32 = jnp.float32
bf16 = jnp.bfloat16


def dot(a, b, ca, cb, precision=highest):
    return lax.dot_general(
        a, b, (((ca,), (cb,)), ((), ())), precision=precision, preferred_element_type=f32
    )


def iota(shape, dim):
    return lax.broadcasted_iota(jnp.int32, shape, dim)


def split3(x):
    hi = x.astype(bf16)
    rest = x - hi.astype(f32)
    mid = rest.astype(bf16)
    low = (rest - mid.astype(f32)).astype(bf16)
    return hi, mid, low


def prior_kernel(first_ref, half_ref, *refs):
    inputs, (keep_ref, send_ref, aux_ref), held, arrived = (
        refs[:9], refs[9:12], refs[12:21], refs[21]
    )
    copies = [
        pltpu.make_async_copy(source, target, arrived.at[i])
        for i, (source, target) in enumerate(zip(inputs, held))
    ]
    for copy in copies:
        copy.start()
    for copy in copies[:-1]:
        copy.wait()
    (down_ref, across_ref, home_ref, height_ref, order_ref, place_ref, amount_ref, noise_ref,
     state_ref) = held
    members, levels, regions, pixels = state_ref.shape
    batches, size = order_ref.shape
    count = batches * size
    channels = height_ref.shape[1]
    sites = (TILE // STRIDE) * (TILE // STRIDE)

    lane = iota((1, count), 1)
    spread = jnp.where(
        iota((batches, count), 1) // size == iota((batches, count), 0), 1.0, 0.0
    ).astype(f32)
    order = jnp.concatenate([order_ref[k : k + 1] for k in range(batches)], axis=1)
    hit = order == iota((size, count), 0)
    rows = []
    for ref in (place_ref, amount_ref, noise_ref):
        wide = dot(ref[...].astype(f32), spread, 0, 0)
        rows.append(jnp.sum(jnp.where(hit, wide, 0.0), axis=0, keepdims=True))
    aux_ref[...] = jnp.concatenate(rows + [jnp.zeros((SUB - 3, count), f32)], axis=0)

    picked = rows[0].astype(jnp.int32)
    channel = picked // sites
    spot = picked - channel * sites
    spot_row = spot // (TILE // STRIDE)
    spot_col = spot - spot_row * (TILE // STRIDE)
    chosen = jnp.where(iota((channels, count), 0) == channel, 1.0, 0.0).astype(f32)
    heights = dot(height_ref[...], chosen, 1, 0)

    pixel = iota((pixels, 1), 0) + first_ref[0]
    row = pixel // TILE
    col = pixel - row * TILE
    weight_row = jnp.zeros((pixels, 1), f32)
    weight_col = jnp.zeros((pixels, 1), f32)
    for i in range(STRIDE):
        weight_row = jnp.where(row % STRIDE == i, down_ref[i], weight_row)
        weight_col = jnp.where(col % STRIDE == i, across_ref[i], weight_col)
    weight = weight_row * weight_col
    inside = (row // STRIDE == spot_row) & (col // STRIDE == spot_col)
    place = jnp.where(inside, weight, 0.0)

    copies[-1].wait()
    total = jnp.zeros((members * regions, count), f32)
    for level in range(levels):
        grid = state_ref[:, level].astype(f32).reshape(members * regions, pixels).astype(bf16)
        for piece in split3(place * heights[level : level + 1]):
            total = total + dot(grid, piece, 1, 0, None)
    home = jnp.zeros((1, count), jnp.int32)
    for k in range(batches):
        home = jnp.where(lane // size == k, home_ref[k], home)
    here = iota((regions, count), 0) == home
    share = jnp.sum(jnp.where(here[None], total.reshape(members, regions, count), 0.0), axis=1)
    half = keep_ref.shape[0]
    if 2 * half > members:
        share = jnp.concatenate([share, jnp.zeros((2 * half - members, count), f32)], axis=0)
    first = half_ref[0] == 0
    keep_ref[...] = jnp.where(first, share[:half], share[half:])
    send_ref[...] = jnp.where(first, share[half:], share[:half])


def rep(x):
    return jnp.broadcast_to(x, (SUB, x.shape[1]))


def col(x, j):
    return jnp.broadcast_to(x[:, j : j + 1], (SUB, LANES))


def filter_kernel(
    members, own_ref, half_ref, home_ref, radius_ref, mine_ref, other_ref, aux_ref, high_ref, low_ref,
    x_ref, h_ref, b_ref,
):
    padded, count = 2 * mine_ref.shape[0], mine_ref.shape[1]
    batches = home_ref.shape[0]
    size = count // batches
    groups = size // SUB
    channels = radius_ref.shape[0]
    sites = (TILE // STRIDE) * (TILE // STRIDE)
    dof = members - 1.0
    E = padded
    lane = iota((1, LANES), 1)
    member = lane < members

    first = half_ref[0] == 0
    mine, other = mine_ref[...], other_ref[...]
    base = jnp.concatenate(
        [jnp.where(first, mine, other), jnp.where(first, other, mine)], axis=0
    )
    if padded < LANES:
        base = jnp.concatenate([base, jnp.zeros((LANES - padded, count), f32)], axis=0)
    cols = base.T
    aux = aux_ref[...]
    aux_cols = jnp.concatenate([aux, jnp.zeros((LANES - SUB, count), f32)], axis=0).T
    center = jnp.sum(jnp.where(member, cols, 0.0), axis=1, keepdims=True) / members
    x_ref[:count] = jnp.where(
        lane == E, center - aux_cols[:, 1:2], jnp.where(member, cols - center, 0.0)
    )
    square = iota((LANES, LANES), 0)
    x_ref[count:] = jnp.where((square == iota((LANES, LANES), 1)) & (square < members), 1.0, 0.0)

    place = aux_cols[:, 0:1].astype(jnp.int32) // sites
    cut = jnp.zeros((count, 1), f32)
    for c in range(channels):
        cut = jnp.where(place == c, radius_ref[c].astype(f32), cut)
    inverse_cut = 1.0 / (cut + 1.0)
    noise = aux_cols[:, 2:3] * dof

    wide = count + LANES
    owner = jnp.zeros((1, wide), jnp.int32) + own_ref[0]
    for k in range(batches):
        owner = jnp.where(iota((1, wide), 1) // size == k, home_ref[k], owner)

    for b in range(batches):
        r0 = b * size
        xb = x_ref[r0 : r0 + size]
        xm = jnp.where(member, xb, 0.0)
        gram = dot(xm, xm, 1, 1)
        noise_b = noise[r0 : r0 + size]
        gram = gram + jnp.where(iota((size, size), 0) == iota((size, size), 1), noise_b, 0.0)
        G = [gram[SUB * g : SUB * g + SUB] for g in range(groups)]
        X = [xb[SUB * g : SUB * g + SUB] for g in range(groups)]
        for p in range(groups):
            C = [[col(G[g], SUB * p + j) for g in range(p, groups)] for j in range(SUB)]
            s = [[rep(C[j][0][i : i + 1]) for j in range(i + 1)] for i in range(SUB)]
            noise_p = jnp.broadcast_to(noise_b[SUB * p : SUB * p + SUB], (SUB, LANES))
            l = [[None] * SUB for _ in range(SUB)]
            inv = []
            for j in range(SUB):
                inv.append(1.0 / s[j][j])
                for i in range(j + 1, SUB):
                    l[i][j] = s[i][j] * inv[j]
                for i in range(j + 1, SUB):
                    for k in range(j + 1, i + 1):
                        s[i][k] = s[i][k] - l[i][j] * s[k][j]
            U, H, alpha = [], [], []
            for j in range(SUB):
                inv_alpha = 1.0 + jnp.sqrt(rep(noise_p[j : j + 1]) * inv[j])
                alpha.append(1.0 / inv_alpha)
                u = rep(G[p][j : j + 1])
                h = rep(X[p][j : j + 1])
                for i in range(j):
                    u = u - l[j][i][:, :size] * U[i]
                    h = h - (l[j][i] * alpha[i]) * H[i]
                h = jnp.where(lane == E, h * inv_alpha, h)
                U.append(u)
                H.append(h)
                row = jnp.where(lane == E + 1, alpha[j] * inv[j], h)
                h_ref[SUB * p + j : SUB * p + j + 1] = row[:1]
            for g in range(p + 1, groups):
                L = []
                for j in range(SUB):
                    c = C[j][g - p]
                    for i in range(j):
                        c = c - L[i] * s[j][i]
                    L.append(c * inv[j])
                for j in range(SUB):
                    G[g] = G[g] - L[j][:, :size] * U[j]
                    X[g] = X[g] - (L[j] * alpha[j]) * H[j]

        low = min((r0 + size) // LANES * LANES, count)
        span = wide - low
        hb = h_ref[...]
        hm = jnp.where(member, hb, 0.0)
        overlap = dot(hm, hm, 1, 1)
        xr = x_ref[low:]
        W = dot(hm, xr, 1, 1)
        far = jnp.abs(owner[:, low:] - home_ref[b]).astype(f32)
        taper = jnp.maximum(0.0, 1.0 - far * inverse_cut[r0 : r0 + size]) * hb[:, E + 1 : E + 2]
        S = [overlap[SUB * g : SUB * g + SUB] for g in range(groups)]
        W = [W[SUB * g : SUB * g + SUB] for g in range(groups)]
        tiles = span // LANES

        def scale(c, row):
            return jnp.concatenate(
                [c * row[:, LANES * t : LANES * t + LANES] for t in range(tiles)], axis=1
            )

        for p in range(groups):
            C = [[col(S[g], SUB * p + j) for g in range(p, groups)] for j in range(SUB)]
            B = []
            for j in range(SUB):
                w = rep(W[p][j : j + 1])
                for i in range(j):
                    w = w - scale(rep(C[i][0][j : j + 1]), B[i])
                beta = w * rep(taper[SUB * p + j : SUB * p + j + 1])
                B.append(beta)
                b_ref[SUB * p + j : SUB * p + j + 1, low:] = beta[:1]
            for g in range(p + 1, groups):
                for j in range(SUB):
                    W[g] = W[g] - scale(C[j][g - p], B[j])
        x_ref[low:] = xr - dot(b_ref[:, low:], hb, 0, 0)

    last = x_ref[count : count + members]
    mixing = jnp.where(member, last + last[:, E : E + 1], 0.0)
    mixing = mixing - jnp.sum(mixing, axis=0, keepdims=True) / members + 1.0 / members
    high = mixing.astype(bf16)
    high_ref[...] = high
    low_ref[...] = (mixing - high.astype(f32)).astype(bf16)


BOTH = ("region", "lev")


def swap(x, devices, k):
    return lax.ppermute(x, BOTH, [(i, i ^ k) for i in range(devices)])


def exchange(keep, send, state, devices):
    total = keep + swap(send, devices, 1)
    bit = 2
    while bit < devices:
        last = 4 * bit >= devices
        steps = (bit, 2 * bit, 3 * bit) if 2 * bit < devices else (bit,)
        if bit == 2:
            total, state = lax.optimization_barrier((total, state))
            state = jnp.transpose(state, (2, 1, 0, 3))
        if last:
            total, state = lax.optimization_barrier((total, state))
            moved = [swap(total, devices, k) for k in steps]
            whole = lax.all_to_all(
                state, "region", split_axis=0, concat_axis=0, tiled=True
            )
        else:
            moved = [swap(total, devices, k) for k in steps]
        total = total + sum(moved)
        bit *= 4
    return total, swap(total, devices, 1), whole


def body(
    region_count,
    level_count,
    background_members,
    channel_height_kernel,
    sensor_spread_down,
    sensor_spread_across,
    measurement_placement,
    measurement_ordering,
    group_area_number,
    taper_radius_limit,
    measured_amounts,
    measurement_noise_spread,
):
    members, levels, pixels, regions = background_members.shape
    batches, size = measurement_ordering.shape
    count = batches * size
    own_region = lax.axis_index("region").astype(jnp.int32)

    state = jnp.transpose(background_members, (0, 1, 3, 2))
    if regions > 8:
        local = jnp.take(state, group_area_number, axis=2)
        home = jnp.arange(batches, dtype=jnp.int32)
    else:
        local, home = state, group_area_number
    half = -(-members // (2 * SUB)) * SUB
    devices = region_count * level_count
    side = ((own_region * level_count + lax.axis_index("lev")) % 2).astype(jnp.int32)[None]
    vmem = pl.BlockSpec(memory_space=pltpu.VMEM)
    smem = pl.BlockSpec(memory_space=pltpu.SMEM)
    scalars = (sensor_spread_down, sensor_spread_across, home)
    tables = (
        jnp.transpose(channel_height_kernel),
        measurement_ordering,
        measurement_placement,
        measured_amounts,
        measurement_noise_spread,
        local,
    )
    keep, send, aux = pl.pallas_call(
        prior_kernel,
        out_shape=(
            jax.ShapeDtypeStruct((half, count), f32),
            jax.ShapeDtypeStruct((half, count), f32),
            jax.ShapeDtypeStruct((SUB, count), f32),
        ),
        in_specs=[smem] * 2 + [pl.BlockSpec(memory_space=pltpu.HBM)] * 9,
        out_specs=(vmem, vmem, vmem),
        scratch_shapes=[pltpu.SMEM(x.shape, x.dtype) for x in scalars]
        + [pltpu.VMEM(x.shape, x.dtype) for x in tables]
        + [pltpu.SemaphoreType.DMA((9,))],
        compiler_params=pltpu.CompilerParams(vmem_limit_bytes=24 * 2**20),
    )(
        (own_region * pixels)[None],
        side,
        *[pltpu.with_memory_space_constraint(x, pltpu.HBM) for x in (*scalars, *tables)],
    )
    mine, other, whole = exchange(keep, send, state, devices)
    pieces = pl.pallas_call(
        functools.partial(filter_kernel, members),
        out_shape=[jax.ShapeDtypeStruct((members, LANES), bf16)] * 2,
        in_specs=[smem] * 4 + [vmem] * 3,
        out_specs=[vmem, vmem],
        scratch_shapes=[
            pltpu.VMEM((count + LANES, LANES), f32),
            pltpu.VMEM((size, LANES), f32),
            pltpu.VMEM((size, count + LANES), f32),
        ],
        compiler_params=pltpu.CompilerParams(vmem_limit_bytes=16 * 2**20),
        cost_estimate=pl.CostEstimate(flops=10**9, bytes_accessed=10**6, transcendentals=0),
    )(own_region[None], side, group_area_number, taper_radius_limit, mine, other, aux)

    field = jnp.transpose(whole, (2, 1, 0, 3)).reshape(members, -1)
    result = sum(dot(piece[:, :members], field, 0, 0, None) for piece in pieces)
    return result.reshape(members, levels, 1, pixels * region_count).astype(bf16)


def solution(mesh):
    return jax.shard_map(
        functools.partial(body, mesh.shape["region"], mesh.shape["lev"]),
        mesh=mesh,
        in_specs=(
            P(None, "lev", "region", None),
            P(None, "lev"),
            P(),
            P(),
            P(),
            P(),
            P(),
            P(),
            P(),
            P(),
        ),
        out_specs=P(None, "lev", "region", None),
        check_vma=False,
    )
```

```python
import functools

import jax
import jax.numpy as jnp
from jax import lax
from jax.experimental import pallas as pl
from jax.experimental.pallas import tpu as pltpu
from jax.sharding import PartitionSpec as P


TILE = 32
STRIDE = 4
LANES = 128
SUB = 8

highest = lax.Precision.HIGHEST
f32 = jnp.float32
bf16 = jnp.bfloat16


def dot(a, b, ca, cb, precision=highest):
    return lax.dot_general(
        a, b, (((ca,), (cb,)), ((), ())), precision=precision, preferred_element_type=f32
    )


def dot3(a, b, ca, cb):
    a_hi, b_hi = a.astype(bf16), b.astype(bf16)
    a_lo, b_lo = (a - a_hi.astype(f32)).astype(bf16), (b - b_hi.astype(f32)).astype(bf16)
    return dot(a_hi, b_hi, ca, cb, None) + (
        dot(a_hi, b_lo, ca, cb, None) + dot(a_lo, b_hi, ca, cb, None)
    )


def iota(shape, dim):
    return lax.broadcasted_iota(jnp.int32, shape, dim)


def split3(x):
    hi = x.astype(bf16)
    rest = x - hi.astype(f32)
    mid = rest.astype(bf16)
    low = (rest - mid.astype(f32)).astype(bf16)
    return hi, mid, low


def prior_kernel(first_ref, half_ref, *refs):
    inputs, (keep_ref, send_ref, aux_ref), held, arrived = (
        refs[:9], refs[9:12], refs[12:21], refs[21]
    )
    copies = [
        pltpu.make_async_copy(source, target, arrived.at[i])
        for i, (source, target) in enumerate(zip(inputs, held))
    ]
    for copy in copies:
        copy.start()
    for copy in copies[:-1]:
        copy.wait()
    (down_ref, across_ref, home_ref, height_ref, order_ref, place_ref, amount_ref, noise_ref,
     state_ref) = held
    members, levels, regions, pixels = state_ref.shape
    batches, size = order_ref.shape
    count = batches * size
    channels = height_ref.shape[1]
    sites = (TILE // STRIDE) * (TILE // STRIDE)

    lane = iota((1, count), 1)
    spread = jnp.where(
        iota((batches, count), 1) // size == iota((batches, count), 0), 1.0, 0.0
    ).astype(f32)
    order = jnp.concatenate([order_ref[k : k + 1] for k in range(batches)], axis=1)
    hit = order == iota((size, count), 0)
    rows = []
    for ref in (place_ref, amount_ref, noise_ref):
        wide = dot(ref[...].astype(f32), spread, 0, 0)
        rows.append(jnp.sum(jnp.where(hit, wide, 0.0), axis=0, keepdims=True))
    aux_ref[...] = jnp.concatenate(rows + [jnp.zeros((SUB - 3, count), f32)], axis=0)

    picked = rows[0].astype(jnp.int32)
    channel = picked // sites
    spot = picked - channel * sites
    spot_row = spot // (TILE // STRIDE)
    spot_col = spot - spot_row * (TILE // STRIDE)
    chosen = jnp.where(iota((channels, count), 0) == channel, 1.0, 0.0).astype(f32)
    heights = dot(height_ref[...], chosen, 1, 0)

    pixel = iota((pixels, 1), 0) + first_ref[0]
    row = pixel // TILE
    col = pixel - row * TILE
    weight_row = jnp.zeros((pixels, 1), f32)
    weight_col = jnp.zeros((pixels, 1), f32)
    for i in range(STRIDE):
        weight_row = jnp.where(row % STRIDE == i, down_ref[i], weight_row)
        weight_col = jnp.where(col % STRIDE == i, across_ref[i], weight_col)
    weight = weight_row * weight_col
    inside = (row // STRIDE == spot_row) & (col // STRIDE == spot_col)
    place = jnp.where(inside, weight, 0.0)

    copies[-1].wait()
    total = jnp.zeros((members * regions, count), f32)
    for level in range(levels):
        grid = state_ref[:, level].astype(f32).reshape(members * regions, pixels).astype(bf16)
        for piece in split3(place * heights[level : level + 1]):
            total = total + dot(grid, piece, 1, 0, None)
    home = jnp.zeros((1, count), jnp.int32)
    for k in range(batches):
        home = jnp.where(lane // size == k, home_ref[k], home)
    here = iota((regions, count), 0) == home
    share = jnp.sum(jnp.where(here[None], total.reshape(members, regions, count), 0.0), axis=1)
    half = keep_ref.shape[0]
    if 2 * half > members:
        share = jnp.concatenate([share, jnp.zeros((2 * half - members, count), f32)], axis=0)
    first = half_ref[0] == 0
    keep_ref[...] = jnp.where(first, share[:half], share[half:])
    send_ref[...] = jnp.where(first, share[half:], share[:half])


def rep(x):
    return jnp.broadcast_to(x, (SUB, x.shape[1]))


def col(x, j):
    if x.shape[1] < LANES:
        x = jnp.concatenate([x, jnp.zeros((SUB, LANES - x.shape[1]), f32)], axis=1)
    return jnp.take_along_axis(x, jnp.full((SUB, LANES), j, jnp.int32), axis=1)


def filter_kernel(
    members, own_ref, half_ref, home_ref, radius_ref, mine_ref, other_ref, aux_ref, high_ref, low_ref,
    x_ref, h_ref, b_ref, row_ref, pair_ref,
):
    padded, count = 2 * mine_ref.shape[0], mine_ref.shape[1]
    batches = home_ref.shape[0]
    size = count // batches
    groups = size // SUB
    channels = radius_ref.shape[0]
    sites = (TILE // STRIDE) * (TILE // STRIDE)
    dof = members - 1.0
    E = padded
    lane = iota((1, LANES), 1)
    member = lane < members

    first = half_ref[0] == 0
    mine, other = mine_ref[...], other_ref[...]
    base = jnp.concatenate(
        [jnp.where(first, mine, other), jnp.where(first, other, mine)], axis=0
    )
    if padded < LANES:
        base = jnp.concatenate([base, jnp.zeros((LANES - padded, count), f32)], axis=0)
    cols = base.T
    aux = aux_ref[...]
    aux_cols = jnp.concatenate([aux, jnp.zeros((LANES - SUB, count), f32)], axis=0).T
    center = jnp.sum(jnp.where(member, cols, 0.0), axis=1, keepdims=True) / members
    x_ref[:count] = jnp.where(
        lane == E, center - aux_cols[:, 1:2], jnp.where(member, cols - center, 0.0)
    )
    square = iota((LANES, LANES), 0)
    x_ref[count:] = jnp.where((square == iota((LANES, LANES), 1)) & (square < members), 1.0, 0.0)

    place = aux_cols[:, 0:1].astype(jnp.int32) // sites
    cut = jnp.zeros((count, 1), f32)
    for c in range(channels):
        cut = jnp.where(place == c, radius_ref[c].astype(f32), cut)
    inverse_cut = 1.0 / (cut + 1.0)
    noise = aux_cols[:, 2:3] * dof

    wide = count + LANES
    owner = jnp.zeros((1, wide), jnp.int32) + own_ref[0]
    for k in range(batches):
        owner = jnp.where(iota((1, wide), 1) // size == k, home_ref[k], owner)

    for b in range(batches):
        r0 = b * size
        xb = x_ref[r0 : r0 + size]
        xm = jnp.where(member, xb, 0.0)
        gram = dot(xm, xm, 1, 1)
        noise_b = noise[r0 : r0 + size]
        gram = gram + jnp.where(iota((size, size), 0) == iota((size, size), 1), noise_b, 0.0)
        G = [gram[SUB * g : SUB * g + SUB] for g in range(groups)]
        X = [xb[SUB * g : SUB * g + SUB] for g in range(groups)]
        for p in range(groups):
            C = [[col(G[g], SUB * p + j) for g in range(p, groups)] for j in range(SUB)]
            s = [[rep(C[j][0][i : i + 1]) for j in range(i + 1)] for i in range(SUB)]
            noise_p = jnp.broadcast_to(noise_b[SUB * p : SUB * p + SUB], (SUB, LANES))
            l = [[None] * SUB for _ in range(SUB)]
            inv = []
            for j in range(SUB):
                inv.append(1.0 / s[j][j])
                for i in range(j + 1, SUB):
                    l[i][j] = s[i][j] * inv[j]
                for i in range(j + 1, SUB):
                    for k in range(j + 1, i + 1):
                        s[i][k] = s[i][k] - l[i][j] * s[k][j]
            U, alpha = [], []
            scaled = []
            pair_ref[:, :size] = G[p]
            pair_ref[:, LANES:] = X[p]
            for j in range(SUB):
                share = rep(noise_p[j : j + 1]) * inv[j]
                inv_alpha = 1.0 + share * lax.rsqrt(share)
                alpha.append(1.0 / inv_alpha)
                u = rep(pair_ref[j : j + 1, :size])
                h = rep(pair_ref[j : j + 1, LANES:])
                for i in range(j):
                    u = u - l[j][i][:, :size] * U[i]
                    h = h - l[j][i] * scaled[i]
                h = jnp.where(lane == E, h * inv_alpha, h)
                U.append(u)
                scaled.append(alpha[j] * h)
                row = jnp.where(lane == E + 1, alpha[j] * inv[j], h)
                h_ref[SUB * p + j : SUB * p + j + 1] = row[:1]
            for g in range(p + 1, groups):
                L = []
                for j in range(SUB):
                    c = C[j][g - p]
                    for i in range(j):
                        c = c - L[i] * s[j][i]
                    L.append(c * inv[j])
                for j in range(SUB):
                    G[g] = G[g] - L[j][:, :size] * U[j]
                    X[g] = X[g] - L[j] * scaled[j]

        low = min((r0 + size) // LANES * LANES, count)
        span = wide - low
        hb = h_ref[...]
        hm = jnp.where(member, hb, 0.0)
        overlap = dot3(hm, hm, 1, 1)
        xr = x_ref[low:]
        W = dot3(hm, xr, 1, 1)
        far = jnp.abs(owner[:, low:] - home_ref[b]).astype(f32)
        taper = jnp.maximum(0.0, 1.0 - far * inverse_cut[r0 : r0 + size]) * hb[:, E + 1 : E + 2]
        S = [overlap[SUB * g : SUB * g + SUB] for g in range(groups)]
        W = [W[SUB * g : SUB * g + SUB] for g in range(groups)]
        tiles = span // LANES

        def scale(c, row):
            return jnp.concatenate(
                [c * row[:, LANES * t : LANES * t + LANES] for t in range(tiles)], axis=1
            )

        for p in range(groups):
            C = [[col(S[g], SUB * p + j) for g in range(p, groups)] for j in range(SUB)]
            B = []
            row_ref[:, : LANES * tiles] = W[p]
            for j in range(SUB):
                w = rep(row_ref[j : j + 1, : LANES * tiles])
                for i in range(j):
                    w = w - scale(rep(C[i][0][j : j + 1]), B[i])
                beta = w * rep(taper[SUB * p + j : SUB * p + j + 1])
                B.append(beta)
                b_ref[SUB * p + j : SUB * p + j + 1, low:] = beta[:1]
            for g in range(p + 1, groups):
                for j in range(SUB):
                    W[g] = W[g] - scale(C[j][g - p], B[j])
        x_ref[low:] = xr - dot3(b_ref[:, low:], hb, 0, 0)

    last = x_ref[count : count + members]
    mixing = jnp.where(member, last + last[:, E : E + 1], 0.0)
    mixing = mixing - jnp.sum(mixing, axis=0, keepdims=True) / members + 1.0 / members
    high = mixing.astype(bf16)
    high_ref[...] = high
    low_ref[...] = (mixing - high.astype(f32)).astype(bf16)


BOTH = ("region", "lev")


def swap(x, devices, k):
    return lax.ppermute(x, BOTH, [(i, i ^ k) for i in range(devices)])


def exchange(keep, send, state, devices):
    total = keep + swap(send, devices, 1)
    total, state = lax.optimization_barrier((total, state))
    state = jnp.transpose(state, (2, 1, 0, 3))
    bit = 2
    while bit < devices:
        steps = (bit, 2 * bit, 3 * bit) if 2 * bit < devices else (bit,)
        moved = [swap(total, devices, k) for k in steps]
        total = total + sum(moved)
        bit *= 4
    whole = lax.all_to_all(state, "region", split_axis=0, concat_axis=0, tiled=True)
    return total, swap(total, devices, 1), whole


def body(
    region_count,
    level_count,
    background_members,
    channel_height_kernel,
    sensor_spread_down,
    sensor_spread_across,
    measurement_placement,
    measurement_ordering,
    group_area_number,
    taper_radius_limit,
    measured_amounts,
    measurement_noise_spread,
):
    members, levels, pixels, regions = background_members.shape
    batches, size = measurement_ordering.shape
    count = batches * size
    own_region = lax.axis_index("region").astype(jnp.int32)

    state = jnp.transpose(background_members, (0, 1, 3, 2))
    if regions > 8:
        local = jnp.take(state, group_area_number, axis=2)
        home = jnp.arange(batches, dtype=jnp.int32)
    else:
        local, home = state, group_area_number
    half = -(-members // (2 * SUB)) * SUB
    devices = region_count * level_count
    side = ((own_region * level_count + lax.axis_index("lev")) % 2).astype(jnp.int32)[None]
    vmem = pl.BlockSpec(memory_space=pltpu.VMEM)
    smem = pl.BlockSpec(memory_space=pltpu.SMEM)
    scalars = (sensor_spread_down, sensor_spread_across, home)
    tables = (
        jnp.transpose(channel_height_kernel),
        measurement_ordering,
        measurement_placement,
        measured_amounts,
        measurement_noise_spread,
        local,
    )
    keep, send, aux = pl.pallas_call(
        prior_kernel,
        out_shape=(
            jax.ShapeDtypeStruct((half, count), f32),
            jax.ShapeDtypeStruct((half, count), f32),
            jax.ShapeDtypeStruct((SUB, count), f32),
        ),
        in_specs=[smem] * 2 + [pl.BlockSpec(memory_space=pltpu.HBM)] * 9,
        out_specs=(vmem, vmem, vmem),
        scratch_shapes=[pltpu.SMEM(x.shape, x.dtype) for x in scalars]
        + [pltpu.VMEM(x.shape, x.dtype) for x in tables]
        + [pltpu.SemaphoreType.DMA((9,))],
        compiler_params=pltpu.CompilerParams(vmem_limit_bytes=24 * 2**20),
    )(
        (own_region * pixels)[None],
        side,
        *[pltpu.with_memory_space_constraint(x, pltpu.HBM) for x in (*scalars, *tables)],
    )
    mine, other, whole = exchange(keep, send, state, devices)
    pieces = pl.pallas_call(
        functools.partial(filter_kernel, members),
        out_shape=[jax.ShapeDtypeStruct((members, LANES), bf16)] * 2,
        in_specs=[smem] * 4 + [vmem] * 3,
        out_specs=[vmem, vmem],
        scratch_shapes=[
            pltpu.VMEM((count + LANES, LANES), f32),
            pltpu.VMEM((size, LANES), f32),
            pltpu.VMEM((size, count + LANES), f32),
            pltpu.VMEM((SUB, count + LANES), f32),
            pltpu.VMEM((SUB, 2 * LANES), f32),
        ],
        compiler_params=pltpu.CompilerParams(vmem_limit_bytes=16 * 2**20),
        cost_estimate=pl.CostEstimate(flops=10**9, bytes_accessed=10**6, transcendentals=0),
    )(own_region[None], side, group_area_number, taper_radius_limit, mine, other, aux)

    field = jnp.transpose(whole, (2, 1, 0, 3)).reshape(members, -1)
    result = sum(dot(piece[:, :members], field, 0, 0, None) for piece in pieces)
    return result.reshape(members, levels, 1, pixels * region_count).astype(bf16)


def solution(mesh):
    return jax.shard_map(
        functools.partial(body, mesh.shape["region"], mesh.shape["lev"]),
        mesh=mesh,
        in_specs=(
            P(None, "lev", "region", None),
            P(None, "lev"),
            P(),
            P(),
            P(),
            P(),
            P(),
            P(),
            P(),
            P(),
        ),
        out_specs=P(None, "lev", "region", None),
        check_vma=False,
    )
```

```python
import functools

import jax
import jax.numpy as jnp
from jax import lax
from jax.experimental import pallas as pl
from jax.experimental.pallas import tpu as pltpu
from jax.sharding import PartitionSpec as P


TILE = 32
STRIDE = 4
LANES = 128
SUB = 8

highest = lax.Precision.HIGHEST
f32 = jnp.float32
bf16 = jnp.bfloat16


def dot(a, b, ca, cb, precision=highest):
    return lax.dot_general(
        a, b, (((ca,), (cb,)), ((), ())), precision=precision, preferred_element_type=f32
    )


def dot3(a, b, ca, cb):
    a_hi, b_hi = a.astype(bf16), b.astype(bf16)
    a_lo, b_lo = (a - a_hi.astype(f32)).astype(bf16), (b - b_hi.astype(f32)).astype(bf16)
    return dot(a_hi, b_hi, ca, cb, None) + (
        dot(a_hi, b_lo, ca, cb, None) + dot(a_lo, b_hi, ca, cb, None)
    )


def iota(shape, dim):
    return lax.broadcasted_iota(jnp.int32, shape, dim)


def split3(x):
    hi = x.astype(bf16)
    rest = x - hi.astype(f32)
    mid = rest.astype(bf16)
    low = (rest - mid.astype(f32)).astype(bf16)
    return hi, mid, low


def prior_kernel(first_ref, half_ref, *refs):
    inputs, (keep_ref, send_ref, aux_ref), held, arrived = (
        refs[:11], refs[11:14], refs[14:25], refs[25]
    )
    copies = [
        pltpu.make_async_copy(source, target, arrived.at[i])
        for i, (source, target) in enumerate(zip(inputs, held))
    ]
    for copy in copies:
        copy.start()
    for copy in copies[:-1]:
        copy.wait()
    (down_ref, across_ref, home_ref, area_ref, radius_ref, height_ref, order_ref, place_ref, amount_ref, noise_ref,
     state_ref) = held
    members, levels, regions, pixels = state_ref.shape
    batches, size = order_ref.shape
    count = batches * size
    channels = height_ref.shape[1]
    sites = (TILE // STRIDE) * (TILE // STRIDE)

    lane = iota((1, count), 1)
    spread = jnp.where(
        iota((batches, count), 1) // size == iota((batches, count), 0), 1.0, 0.0
    ).astype(f32)
    order = jnp.concatenate([order_ref[k : k + 1] for k in range(batches)], axis=1)
    hit = order == iota((size, count), 0)
    rows = []
    for ref in (place_ref, amount_ref, noise_ref):
        wide = dot(ref[...].astype(f32), spread, 0, 0)
        rows.append(jnp.sum(jnp.where(hit, wide, 0.0), axis=0, keepdims=True))
    picked = rows[0].astype(jnp.int32)
    channel = picked // sites
    cut = jnp.zeros((1, count), jnp.int32)
    for c in range(channels):
        cut = jnp.where(channel == c, radius_ref[c], cut)
    area = jnp.zeros((1, count), jnp.int32)
    for k in range(batches):
        area = jnp.where(lane // size == k, area_ref[k], area)
    rows += [cut.astype(f32), area.astype(f32), jnp.zeros((SUB - 5, count), f32)]
    aux_ref[...] = jnp.concatenate(rows, axis=0)
    spot = picked - channel * sites
    spot_row = spot // (TILE // STRIDE)
    spot_col = spot - spot_row * (TILE // STRIDE)
    chosen = jnp.where(iota((channels, count), 0) == channel, 1.0, 0.0).astype(f32)
    heights = dot(height_ref[...], chosen, 1, 0)

    pixel = iota((pixels, 1), 0) + first_ref[0]
    row = pixel // TILE
    col = pixel - row * TILE
    weight_row = jnp.zeros((pixels, 1), f32)
    weight_col = jnp.zeros((pixels, 1), f32)
    for i in range(STRIDE):
        weight_row = jnp.where(row % STRIDE == i, down_ref[i], weight_row)
        weight_col = jnp.where(col % STRIDE == i, across_ref[i], weight_col)
    weight = weight_row * weight_col
    inside = (row // STRIDE == spot_row) & (col // STRIDE == spot_col)
    place = jnp.where(inside, weight, 0.0)

    copies[-1].wait()
    total = jnp.zeros((members * regions, count), f32)
    for level in range(levels):
        grid = state_ref[:, level].astype(f32).reshape(members * regions, pixels).astype(bf16)
        for piece in split3(place * heights[level : level + 1]):
            total = total + dot(grid, piece, 1, 0, None)
    home = jnp.zeros((1, count), jnp.int32)
    for k in range(batches):
        home = jnp.where(lane // size == k, home_ref[k], home)
    here = iota((regions, count), 0) == home
    share = jnp.sum(jnp.where(here[None], total.reshape(members, regions, count), 0.0), axis=1)
    half = keep_ref.shape[0]
    if 2 * half > members:
        share = jnp.concatenate([share, jnp.zeros((2 * half - members, count), f32)], axis=0)
    first = half_ref[0] == 0
    keep_ref[...] = jnp.where(first, share[:half], share[half:])
    send_ref[...] = jnp.where(first, share[half:], share[:half])


def rep(x):
    return jnp.broadcast_to(x, (SUB, x.shape[1]))


def col(x, j):
    if x.shape[1] < LANES:
        x = jnp.concatenate([x, jnp.zeros((SUB, LANES - x.shape[1]), f32)], axis=1)
    return jnp.take_along_axis(x, jnp.full((SUB, LANES), j, jnp.int32), axis=1)


def filter_kernel(
    members, batches, own_ref, half_ref, mine_ref, other_ref, aux_ref, high_ref, low_ref,
    x_ref, h_ref, b_ref, row_ref, pair_ref,
):
    padded, count = 2 * mine_ref.shape[0], mine_ref.shape[1]
    size = count // batches
    groups = size // SUB
    dof = members - 1.0
    E = padded
    lane = iota((1, LANES), 1)
    member = lane < members

    first = half_ref[0] == 0
    mine, other = mine_ref[...], other_ref[...]
    base = jnp.concatenate(
        [jnp.where(first, mine, other), jnp.where(first, other, mine)], axis=0
    )
    if padded < LANES:
        base = jnp.concatenate([base, jnp.zeros((LANES - padded, count), f32)], axis=0)
    cols = base.T
    aux = aux_ref[...]
    aux_cols = jnp.concatenate([aux, jnp.zeros((LANES - SUB, count), f32)], axis=0).T
    center = jnp.sum(jnp.where(member, cols, 0.0), axis=1, keepdims=True) / members
    x_ref[:count] = jnp.where(
        lane == E, center - aux_cols[:, 1:2], jnp.where(member, cols - center, 0.0)
    )
    square = iota((LANES, LANES), 0)
    x_ref[count:] = jnp.where((square == iota((LANES, LANES), 1)) & (square < members), 1.0, 0.0)

    inverse_cut = 1.0 / (aux_cols[:, 3:4] + 1.0)
    noise = aux_cols[:, 2:3] * dof

    wide = count + LANES
    own = jnp.zeros((1, LANES), f32) + own_ref[0].astype(f32)
    owner = jnp.concatenate([aux[4:5], own], axis=1)

    for b in range(batches):
        r0 = b * size
        xb = x_ref[r0 : r0 + size]
        xm = jnp.where(member, xb, 0.0)
        gram = dot(xm, xm, 1, 1)
        noise_b = noise[r0 : r0 + size]
        gram = gram + jnp.where(iota((size, size), 0) == iota((size, size), 1), noise_b, 0.0)
        G = [gram[SUB * g : SUB * g + SUB] for g in range(groups)]
        X = [xb[SUB * g : SUB * g + SUB] for g in range(groups)]
        for p in range(groups):
            C = [[col(G[g], SUB * p + j) for g in range(p, groups)] for j in range(SUB)]
            s = [[rep(C[j][0][i : i + 1]) for j in range(i + 1)] for i in range(SUB)]
            noise_p = jnp.broadcast_to(noise_b[SUB * p : SUB * p + SUB], (SUB, LANES))
            l = [[None] * SUB for _ in range(SUB)]
            inv = []
            for j in range(SUB):
                inv.append(1.0 / s[j][j])
                for i in range(j + 1, SUB):
                    l[i][j] = s[i][j] * inv[j]
                for i in range(j + 1, SUB):
                    for k in range(j + 1, i + 1):
                        s[i][k] = s[i][k] - l[i][j] * s[k][j]
            U, alpha = [], []
            scaled = []
            pair_ref[:, :size] = G[p]
            pair_ref[:, LANES:] = X[p]
            for j in range(SUB):
                share = rep(noise_p[j : j + 1]) * inv[j]
                inv_alpha = 1.0 + share * lax.rsqrt(share)
                alpha.append(1.0 / inv_alpha)
                u = rep(pair_ref[j : j + 1, :size])
                h = rep(pair_ref[j : j + 1, LANES:])
                for i in range(j):
                    u = u - l[j][i][:, :size] * U[i]
                    h = h - l[j][i] * scaled[i]
                h = jnp.where(lane == E, h * inv_alpha, h)
                U.append(u)
                scaled.append(alpha[j] * h)
                row = jnp.where(lane == E + 1, alpha[j] * inv[j], h)
                h_ref[SUB * p + j : SUB * p + j + 1] = row[:1]
            for g in range(p + 1, groups):
                L = []
                for j in range(SUB):
                    c = C[j][g - p]
                    for i in range(j):
                        c = c - L[i] * s[j][i]
                    L.append(c * inv[j])
                for j in range(SUB):
                    G[g] = G[g] - L[j][:, :size] * U[j]
                    X[g] = X[g] - L[j] * scaled[j]

        low = min((r0 + size) // LANES * LANES, count)
        span = wide - low
        hb = h_ref[...]
        hm = jnp.where(member, hb, 0.0)
        overlap = dot3(hm, hm, 1, 1)
        xr = x_ref[low:]
        W = dot3(hm, xr, 1, 1)
        far = jnp.abs(owner[:, low:] - aux_cols[r0 : r0 + size, 4:5])
        taper = jnp.maximum(0.0, 1.0 - far * inverse_cut[r0 : r0 + size]) * hb[:, E + 1 : E + 2]
        S = [overlap[SUB * g : SUB * g + SUB] for g in range(groups)]
        W = [W[SUB * g : SUB * g + SUB] for g in range(groups)]
        tiles = span // LANES

        def scale(c, row):
            return jnp.concatenate(
                [c * row[:, LANES * t : LANES * t + LANES] for t in range(tiles)], axis=1
            )

        for p in range(groups):
            C = [[col(S[g], SUB * p + j) for g in range(p, groups)] for j in range(SUB)]
            B = []
            row_ref[:, : LANES * tiles] = W[p]
            for j in range(SUB):
                w = rep(row_ref[j : j + 1, : LANES * tiles])
                for i in range(j):
                    w = w - scale(rep(C[i][0][j : j + 1]), B[i])
                beta = w * rep(taper[SUB * p + j : SUB * p + j + 1])
                B.append(beta)
                b_ref[SUB * p + j : SUB * p + j + 1, low:] = beta[:1]
            for g in range(p + 1, groups):
                for j in range(SUB):
                    W[g] = W[g] - scale(C[j][g - p], B[j])
        x_ref[low:] = xr - dot3(b_ref[:, low:], hb, 0, 0)

    last = x_ref[count : count + members]
    mixing = jnp.where(member, last + last[:, E : E + 1], 0.0)
    mixing = mixing - jnp.sum(mixing, axis=0, keepdims=True) / members + 1.0 / members
    high = mixing.astype(bf16)
    high_ref[...] = high
    low_ref[...] = (mixing - high.astype(f32)).astype(bf16)


def apply_kernel(high_ref, low_ref, whole_ref, out_ref, row_ref):
    sources, levels, members, pixels = whole_ref.shape
    high, low = high_ref[:, :members], low_ref[:, :members]
    for level in range(levels):
        field = jnp.concatenate([whole_ref[s, level] for s in range(sources)], axis=1)
        value = dot(high, field, 0, 0, None) + dot(low, field, 0, 0, None)
        for s in range(sources):
            part = value[:, pixels * s : pixels * s + pixels]
            row_ref[s, pl.ds(level, members, stride=levels), :] = part
    for s in range(sources):
        part = row_ref[s].reshape(members, levels, pixels).astype(bf16)
        out_ref[:, :, pixels * s : pixels * s + pixels] = part


BOTH = ("region", "lev")


def swap(x, devices, k):
    return lax.ppermute(x, BOTH, [(i, i ^ k) for i in range(devices)])


def exchange(keep, send, state, devices):
    total = keep + swap(send, devices, 1)
    total, state = lax.optimization_barrier((total, state))
    state = jnp.transpose(state, (2, 1, 0, 3))
    stages = []
    bit = 8
    while bit < devices:
        stages.append((3 * bit, 2 * bit, bit) if 2 * bit < devices else (bit,))
        bit *= 4
    stages += [(k,) for k in (4, 2) if k < devices]
    for steps in stages:
        moved = [swap(total, devices, k) for k in steps]
        total = total + sum(moved)
    whole = lax.all_to_all(state, "region", split_axis=0, concat_axis=0, tiled=True)
    return total, swap(total, devices, 1), whole


def body(
    region_count,
    level_count,
    background_members,
    channel_height_kernel,
    sensor_spread_down,
    sensor_spread_across,
    measurement_placement,
    measurement_ordering,
    group_area_number,
    taper_radius_limit,
    measured_amounts,
    measurement_noise_spread,
):
    members, levels, pixels, regions = background_members.shape
    batches, size = measurement_ordering.shape
    count = batches * size
    own_region = lax.axis_index("region").astype(jnp.int32)

    state = jnp.transpose(background_members, (0, 1, 3, 2))
    if regions > 8:
        local = jnp.take(state, group_area_number, axis=2)
        home = jnp.arange(batches, dtype=jnp.int32)
    else:
        local, home = state, group_area_number
    half = -(-members // (2 * SUB)) * SUB
    devices = region_count * level_count
    side = ((own_region * level_count + lax.axis_index("lev")) % 2).astype(jnp.int32)[None]
    vmem = pl.BlockSpec(memory_space=pltpu.VMEM)
    smem = pl.BlockSpec(memory_space=pltpu.SMEM)
    scalars = (
        sensor_spread_down, sensor_spread_across, home, group_area_number, taper_radius_limit
    )
    tables = (
        jnp.transpose(channel_height_kernel),
        measurement_ordering,
        measurement_placement,
        measured_amounts,
        measurement_noise_spread,
        local,
    )
    keep, send, aux = pl.pallas_call(
        prior_kernel,
        out_shape=(
            jax.ShapeDtypeStruct((half, count), f32),
            jax.ShapeDtypeStruct((half, count), f32),
            jax.ShapeDtypeStruct((SUB, count), f32),
        ),
        in_specs=[smem] * 2 + [pl.BlockSpec(memory_space=pltpu.HBM)] * 11,
        out_specs=(vmem, vmem, vmem),
        scratch_shapes=[pltpu.SMEM(x.shape, x.dtype) for x in scalars]
        + [pltpu.VMEM(x.shape, x.dtype) for x in tables]
        + [pltpu.SemaphoreType.DMA((11,))],
        compiler_params=pltpu.CompilerParams(vmem_limit_bytes=24 * 2**20),
    )(
        (own_region * pixels)[None],
        side,
        *[pltpu.with_memory_space_constraint(x, pltpu.HBM) for x in (*scalars, *tables)],
    )
    mine, other, whole = exchange(keep, send, state, devices)
    pieces = pl.pallas_call(
        functools.partial(filter_kernel, members, batches),
        out_shape=[jax.ShapeDtypeStruct((members, LANES), bf16)] * 2,
        in_specs=[smem] * 2 + [vmem] * 3,
        out_specs=[vmem, vmem],
        scratch_shapes=[
            pltpu.VMEM((count + LANES, LANES), f32),
            pltpu.VMEM((size, LANES), f32),
            pltpu.VMEM((size, count + LANES), f32),
            pltpu.VMEM((SUB, count + LANES), f32),
            pltpu.VMEM((SUB, 2 * LANES), f32),
        ],
        compiler_params=pltpu.CompilerParams(vmem_limit_bytes=16 * 2**20),
        cost_estimate=pl.CostEstimate(flops=10**9, bytes_accessed=10**6, transcendentals=0),
    )(own_region[None], side, mine, other, aux)

    if pixels % LANES == 0 and levels == 4:
        result = pl.pallas_call(
            apply_kernel,
            out_shape=jax.ShapeDtypeStruct((members, levels, pixels * region_count), bf16),
            in_specs=[vmem] * 3,
            out_specs=vmem,
            scratch_shapes=[pltpu.VMEM((region_count, members * levels, pixels), f32)],
            compiler_params=pltpu.CompilerParams(vmem_limit_bytes=24 * 2**20),
        )(*pieces, whole)
        return result[:, :, None]
    field = jnp.transpose(whole, (2, 1, 0, 3)).reshape(members, -1)
    result = sum(dot(piece[:, :members], field, 0, 0, None) for piece in pieces)
    return result.reshape(members, levels, 1, pixels * region_count).astype(bf16)


def solution(mesh):
    return jax.shard_map(
        functools.partial(body, mesh.shape["region"], mesh.shape["lev"]),
        mesh=mesh,
        in_specs=(
            P(None, "lev", "region", None),
            P(None, "lev"),
            P(),
            P(),
            P(),
            P(),
            P(),
            P(),
            P(),
            P(),
        ),
        out_specs=P(None, "lev", "region", None),
        check_vma=False,
    )
```

```python
import functools

import jax
import jax.numpy as jnp
from jax import lax
from jax.experimental import pallas as pl
from jax.experimental.pallas import tpu as pltpu
from jax.sharding import PartitionSpec as P


TILE = 32
STRIDE = 4
LANES = 128
SUB = 8

highest = lax.Precision.HIGHEST
f32 = jnp.float32
bf16 = jnp.bfloat16


def dot(a, b, ca, cb, precision=highest):
    return lax.dot_general(
        a, b, (((ca,), (cb,)), ((), ())), precision=precision, preferred_element_type=f32
    )


def dot3(a, b, ca, cb):
    a_hi, b_hi = a.astype(bf16), b.astype(bf16)
    a_lo, b_lo = (a - a_hi.astype(f32)).astype(bf16), (b - b_hi.astype(f32)).astype(bf16)
    return dot(a_hi, b_hi, ca, cb, None) + (
        dot(a_hi, b_lo, ca, cb, None) + dot(a_lo, b_hi, ca, cb, None)
    )


def iota(shape, dim):
    return lax.broadcasted_iota(jnp.int32, shape, dim)


def split3(x):
    hi = x.astype(bf16)
    rest = x - hi.astype(f32)
    mid = rest.astype(bf16)
    low = (rest - mid.astype(f32)).astype(bf16)
    return hi, mid, low


def prior_kernel(first_ref, half_ref, *refs):
    inputs, (keep_ref, send_ref, aux_ref), held, arrived, grid_ref = (
        refs[:11], refs[11:14], refs[14:25], refs[25], refs[26]
    )
    copies = [
        pltpu.make_async_copy(source, target, arrived.at[i])
        for i, (source, target) in enumerate(zip(inputs, held))
    ]
    for copy in copies:
        copy.start()
    for copy in copies[:-1]:
        copy.wait()
    (down_ref, across_ref, home_ref, area_ref, radius_ref, height_ref, order_ref, place_ref, amount_ref, noise_ref,
     state_ref) = held
    members, levels, regions, pixels = state_ref.shape
    batches, size = order_ref.shape
    count = batches * size
    channels = height_ref.shape[1]
    sites = (TILE // STRIDE) * (TILE // STRIDE)

    lane = iota((1, count), 1)
    spread = jnp.where(
        iota((batches, count), 1) // size == iota((batches, count), 0), 1.0, 0.0
    ).astype(f32)
    order = jnp.concatenate([order_ref[k : k + 1] for k in range(batches)], axis=1)
    hit = order == iota((size, count), 0)
    rows = []
    for ref in (place_ref, amount_ref, noise_ref):
        wide = dot(ref[...].astype(f32), spread, 0, 0)
        rows.append(jnp.sum(jnp.where(hit, wide, 0.0), axis=0, keepdims=True))
    picked = rows[0].astype(jnp.int32)
    channel = picked // sites
    cut = jnp.zeros((1, count), jnp.int32)
    for c in range(channels):
        cut = jnp.where(channel == c, radius_ref[c], cut)
    area = jnp.zeros((1, count), jnp.int32)
    for k in range(batches):
        area = jnp.where(lane // size == k, area_ref[k], area)
    rows += [cut.astype(f32), area.astype(f32), jnp.zeros((SUB - 5, count), f32)]
    aux_ref[...] = jnp.concatenate(rows, axis=0)
    spot = picked - channel * sites
    spot_row = spot // (TILE // STRIDE)
    spot_col = spot - spot_row * (TILE // STRIDE)
    chosen = jnp.where(iota((channels, count), 0) == channel, 1.0, 0.0).astype(f32)
    heights = dot(height_ref[...], chosen, 1, 0)

    pixel = iota((pixels, 1), 0) + first_ref[0]
    row = pixel // TILE
    col = pixel - row * TILE
    weight_row = jnp.zeros((pixels, 1), f32)
    weight_col = jnp.zeros((pixels, 1), f32)
    for i in range(STRIDE):
        weight_row = jnp.where(row % STRIDE == i, down_ref[i], weight_row)
        weight_col = jnp.where(col % STRIDE == i, across_ref[i], weight_col)
    weight = weight_row * weight_col
    inside = (row // STRIDE == spot_row) & (col // STRIDE == spot_col)
    place = jnp.where(inside, weight, 0.0)

    weights = [place * heights[level : level + 1] for level in range(levels)]
    copies[-1].wait()
    if pixels == LANES and LANES % size == 0 and count % LANES == 0:
        for level in range(levels):
            grid_ref[level] = state_ref[:, level].astype(f32).reshape(members * regions, pixels)
        together = LANES // size
        tiles = []
        for tile in range(count // LANES):
            heavy = jnp.concatenate(
                [w[:, LANES * tile : LANES * tile + LANES] for w in weights], axis=0
            )
            high = heavy.astype(bf16)
            low = (heavy - high.astype(f32)).astype(bf16)
            rows = []
            for k in range(tile * together, (tile + 1) * together):
                pick = pl.ds(home_ref[k], members, stride=regions)
                parts = [grid_ref[level, pick, :].astype(bf16) for level in range(levels)]
                rows.append(jnp.concatenate(parts, axis=1))
            grid = jnp.concatenate(rows, axis=0)
            value = dot(grid, high, 1, 0, None) + dot(grid, low, 1, 0, None)
            best = value[:members]
            for i in range(1, together):
                mine = iota((1, LANES), 1) // size == i
                best = jnp.where(mine, value[members * i : members * i + members], best)
            tiles.append(best)
        share = jnp.concatenate(tiles, axis=1)
    else:
        total = jnp.zeros((members * regions, count), f32)
        for level in range(levels):
            grid = state_ref[:, level].astype(f32).reshape(members * regions, pixels)
            for piece in split3(weights[level]):
                total = total + dot(grid.astype(bf16), piece, 1, 0, None)
        home = jnp.zeros((1, count), jnp.int32)
        for k in range(batches):
            home = jnp.where(lane // size == k, home_ref[k], home)
        here = iota((regions, count), 0) == home
        total = total.reshape(members, regions, count)
        share = jnp.sum(jnp.where(here[None], total, 0.0), axis=1)
    half = keep_ref.shape[0]
    if 2 * half > members:
        share = jnp.concatenate([share, jnp.zeros((2 * half - members, count), f32)], axis=0)
    first = half_ref[0] == 0
    keep_ref[...] = jnp.where(first, share[:half], share[half:])
    send_ref[...] = jnp.where(first, share[half:], share[:half])


def rep(x):
    return jnp.broadcast_to(x, (SUB, x.shape[1]))


def col(x, j):
    if x.shape[1] < LANES:
        x = jnp.concatenate([x, jnp.zeros((SUB, LANES - x.shape[1]), f32)], axis=1)
    return jnp.take_along_axis(x, jnp.full((SUB, LANES), j, jnp.int32), axis=1)


def filter_kernel(
    members, batches, own_ref, half_ref, mine_ref, other_ref, aux_ref, high_ref, low_ref,
    x_ref, h_ref, b_ref, row_ref, pair_ref,
):
    padded, count = 2 * mine_ref.shape[0], mine_ref.shape[1]
    size = count // batches
    groups = size // SUB
    dof = members - 1.0
    E = padded
    lane = iota((1, LANES), 1)
    member = lane < members

    first = half_ref[0] == 0
    mine, other = mine_ref[...], other_ref[...]
    base = jnp.concatenate(
        [jnp.where(first, mine, other), jnp.where(first, other, mine)], axis=0
    )
    if padded < LANES:
        base = jnp.concatenate([base, jnp.zeros((LANES - padded, count), f32)], axis=0)
    cols = base.T
    aux = aux_ref[...]
    aux_cols = jnp.concatenate([aux, jnp.zeros((LANES - SUB, count), f32)], axis=0).T
    center = jnp.sum(jnp.where(member, cols, 0.0), axis=1, keepdims=True) / members
    x_ref[:count] = jnp.where(
        lane == E, center - aux_cols[:, 1:2], jnp.where(member, cols - center, 0.0)
    )
    square = iota((LANES, LANES), 0)
    x_ref[count:] = jnp.where((square == iota((LANES, LANES), 1)) & (square < members), 1.0, 0.0)

    inverse_cut = 1.0 / (aux_cols[:, 3:4] + 1.0)
    noise = aux_cols[:, 2:3] * dof

    wide = count + LANES
    own = jnp.zeros((1, LANES), f32) + own_ref[0].astype(f32)
    owner = jnp.concatenate([aux[4:5], own], axis=1)

    for b in range(batches):
        r0 = b * size
        xb = x_ref[r0 : r0 + size]
        xm = jnp.where(member, xb, 0.0)
        gram = dot(xm, xm, 1, 1)
        noise_b = noise[r0 : r0 + size]
        gram = gram + jnp.where(iota((size, size), 0) == iota((size, size), 1), noise_b, 0.0)
        G = [gram[SUB * g : SUB * g + SUB] for g in range(groups)]
        X = [xb[SUB * g : SUB * g + SUB] for g in range(groups)]
        for p in range(groups):
            C = [[col(G[g], SUB * p + j) for g in range(p, groups)] for j in range(SUB)]
            s = [[rep(C[j][0][i : i + 1]) for j in range(i + 1)] for i in range(SUB)]
            noise_p = jnp.broadcast_to(noise_b[SUB * p : SUB * p + SUB], (SUB, LANES))
            l = [[None] * SUB for _ in range(SUB)]
            inv = []
            for j in range(SUB):
                inv.append(1.0 / s[j][j])
                for i in range(j + 1, SUB):
                    l[i][j] = s[i][j] * inv[j]
                for i in range(j + 1, SUB):
                    for k in range(j + 1, i + 1):
                        s[i][k] = s[i][k] - l[i][j] * s[k][j]
            U, alpha = [], []
            scaled = []
            pair_ref[:, :size] = G[p]
            pair_ref[:, LANES:] = X[p]
            for j in range(SUB):
                share = rep(noise_p[j : j + 1]) * inv[j]
                inv_alpha = 1.0 + share * lax.rsqrt(share)
                alpha.append(1.0 / inv_alpha)
                u = rep(pair_ref[j : j + 1, :size])
                h = rep(pair_ref[j : j + 1, LANES:])
                for i in range(j):
                    u = u - l[j][i][:, :size] * U[i]
                    h = h - l[j][i] * scaled[i]
                h = jnp.where(lane == E, h * inv_alpha, h)
                U.append(u)
                scaled.append(alpha[j] * h)
                row = jnp.where(lane == E + 1, alpha[j] * inv[j], h)
                h_ref[SUB * p + j : SUB * p + j + 1] = row[:1]
            for g in range(p + 1, groups):
                L = []
                for j in range(SUB):
                    c = C[j][g - p]
                    for i in range(j):
                        c = c - L[i] * s[j][i]
                    L.append(c * inv[j])
                for j in range(SUB):
                    G[g] = G[g] - L[j][:, :size] * U[j]
                    X[g] = X[g] - L[j] * scaled[j]

        low = min((r0 + size) // LANES * LANES, count)
        span = wide - low
        hb = h_ref[...]
        hm = jnp.where(member, hb, 0.0)
        overlap = dot3(hm, hm, 1, 1)
        xr = x_ref[low:]
        W = dot3(hm, xr, 1, 1)
        far = jnp.abs(owner[:, low:] - aux_cols[r0 : r0 + size, 4:5])
        taper = jnp.maximum(0.0, 1.0 - far * inverse_cut[r0 : r0 + size]) * hb[:, E + 1 : E + 2]
        S = [overlap[SUB * g : SUB * g + SUB] for g in range(groups)]
        W = [W[SUB * g : SUB * g + SUB] for g in range(groups)]
        tiles = span // LANES

        def scale(c, row):
            return jnp.concatenate(
                [c * row[:, LANES * t : LANES * t + LANES] for t in range(tiles)], axis=1
            )

        for p in range(groups):
            C = [[col(S[g], SUB * p + j) for g in range(p, groups)] for j in range(SUB)]
            B = []
            row_ref[:, : LANES * tiles] = W[p]
            for j in range(SUB):
                w = rep(row_ref[j : j + 1, : LANES * tiles])
                for i in range(j):
                    w = w - scale(rep(C[i][0][j : j + 1]), B[i])
                beta = w * rep(taper[SUB * p + j : SUB * p + j + 1])
                B.append(beta)
                b_ref[SUB * p + j : SUB * p + j + 1, low:] = beta[:1]
            for g in range(p + 1, groups):
                for j in range(SUB):
                    W[g] = W[g] - scale(C[j][g - p], B[j])
        x_ref[low:] = xr - dot3(b_ref[:, low:], hb, 0, 0)

    last = x_ref[count : count + members]
    mixing = jnp.where(member, last + last[:, E : E + 1], 0.0)
    mixing = mixing - jnp.sum(mixing, axis=0, keepdims=True) / members + 1.0 / members
    high = mixing.astype(bf16)
    high_ref[...] = high
    low_ref[...] = (mixing - high.astype(f32)).astype(bf16)


def apply_kernel(high_ref, low_ref, whole_ref, out_ref, row_ref, stage_ref, sent):
    sources, levels, members, pixels = whole_ref.shape
    high, low = high_ref[:, :members], low_ref[:, :members]
    parts = sent.shape[0]
    each = sources // parts
    copies = []
    for part in range(parts):
        group = range(part * each, part * each + each)
        for level in range(levels):
            field = jnp.concatenate([whole_ref[s, level] for s in group], axis=1)
            value = dot(high, field, 0, 0, None) + dot(low, field, 0, 0, None)
            for i, s in enumerate(group):
                piece = value[:, pixels * i : pixels * i + pixels]
                row_ref[s, pl.ds(level, members, stride=levels), :] = piece
        for s in group:
            piece = row_ref[s].reshape(members, levels, pixels).astype(bf16)
            stage_ref[:, :, pixels * s : pixels * s + pixels] = piece
        span = pl.ds(part * each * pixels, each * pixels)
        copies.append(
            pltpu.make_async_copy(stage_ref.at[:, :, span], out_ref.at[:, :, span], sent.at[part])
        )
        copies[-1].start()
    for copy in copies:
        copy.wait()


BOTH = ("region", "lev")


def swap(x, devices, k):
    return lax.ppermute(x, BOTH, [(i, i ^ k) for i in range(devices)])


def exchange(keep, send, state, devices):
    total = keep + swap(send, devices, 1)
    total, state = lax.optimization_barrier((total, state))
    state = jnp.transpose(state, (2, 1, 0, 3))
    stages = []
    bit = 8
    while bit < devices:
        stages.append((3 * bit, 2 * bit, bit) if 2 * bit < devices else (bit,))
        bit *= 4
    stages += [(k,) for k in (4, 2) if k < devices]
    for steps in stages:
        moved = [swap(total, devices, k) for k in steps]
        total = total + sum(moved)
    whole = lax.all_to_all(state, "region", split_axis=0, concat_axis=0, tiled=True)
    return total, swap(total, devices, 1), whole


def body(
    region_count,
    level_count,
    background_members,
    channel_height_kernel,
    sensor_spread_down,
    sensor_spread_across,
    measurement_placement,
    measurement_ordering,
    group_area_number,
    taper_radius_limit,
    measured_amounts,
    measurement_noise_spread,
):
    members, levels, pixels, regions = background_members.shape
    batches, size = measurement_ordering.shape
    count = batches * size
    own_region = lax.axis_index("region").astype(jnp.int32)

    state = jnp.transpose(background_members, (0, 1, 3, 2))
    if regions > 8:
        local = jnp.take(state, group_area_number, axis=2)
        home = jnp.arange(batches, dtype=jnp.int32)
    else:
        local, home = state, group_area_number
    half = -(-members // (2 * SUB)) * SUB
    devices = region_count * level_count
    side = ((own_region * level_count + lax.axis_index("lev")) % 2).astype(jnp.int32)[None]
    vmem = pl.BlockSpec(memory_space=pltpu.VMEM)
    smem = pl.BlockSpec(memory_space=pltpu.SMEM)
    scalars = (
        sensor_spread_down, sensor_spread_across, home, group_area_number, taper_radius_limit
    )
    tables = (
        jnp.transpose(channel_height_kernel),
        measurement_ordering,
        measurement_placement,
        measured_amounts,
        measurement_noise_spread,
        local,
    )
    keep, send, aux = pl.pallas_call(
        prior_kernel,
        out_shape=(
            jax.ShapeDtypeStruct((half, count), f32),
            jax.ShapeDtypeStruct((half, count), f32),
            jax.ShapeDtypeStruct((SUB, count), f32),
        ),
        in_specs=[smem] * 2 + [pl.BlockSpec(memory_space=pltpu.HBM)] * 11,
        out_specs=(vmem, vmem, vmem),
        scratch_shapes=[pltpu.SMEM(x.shape, x.dtype) for x in scalars]
        + [pltpu.VMEM(x.shape, x.dtype) for x in tables]
        + [
            pltpu.SemaphoreType.DMA((11,)),
            pltpu.VMEM((levels, members * local.shape[2], pixels), f32),
        ],
        compiler_params=pltpu.CompilerParams(vmem_limit_bytes=24 * 2**20),
    )(
        (own_region * pixels)[None],
        side,
        *[pltpu.with_memory_space_constraint(x, pltpu.HBM) for x in (*scalars, *tables)],
    )
    mine, other, whole = exchange(keep, send, state, devices)
    pieces = pl.pallas_call(
        functools.partial(filter_kernel, members, batches),
        out_shape=[jax.ShapeDtypeStruct((members, LANES), bf16)] * 2,
        in_specs=[smem] * 2 + [vmem] * 3,
        out_specs=[vmem, vmem],
        scratch_shapes=[
            pltpu.VMEM((count + LANES, LANES), f32),
            pltpu.VMEM((size, LANES), f32),
            pltpu.VMEM((size, count + LANES), f32),
            pltpu.VMEM((SUB, count + LANES), f32),
            pltpu.VMEM((SUB, 2 * LANES), f32),
        ],
        compiler_params=pltpu.CompilerParams(vmem_limit_bytes=16 * 2**20),
        cost_estimate=pl.CostEstimate(flops=10**9, bytes_accessed=10**6, transcendentals=0),
    )(own_region[None], side, mine, other, aux)

    if pixels % LANES == 0 and levels == 4:
        result = pl.pallas_call(
            apply_kernel,
            out_shape=jax.ShapeDtypeStruct((members, levels, pixels * region_count), bf16),
            in_specs=[vmem] * 3,
            out_specs=pl.BlockSpec(memory_space=pltpu.HBM),
            scratch_shapes=[
                pltpu.VMEM((region_count, members * levels, pixels), f32),
                pltpu.VMEM((members, levels, pixels * region_count), bf16),
                pltpu.SemaphoreType.DMA((2 if region_count % 2 == 0 else 1,)),
            ],
            compiler_params=pltpu.CompilerParams(vmem_limit_bytes=24 * 2**20),
        )(*pieces, whole)
        return result[:, :, None]
    field = jnp.transpose(whole, (2, 1, 0, 3)).reshape(members, -1)
    result = sum(dot(piece[:, :members], field, 0, 0, None) for piece in pieces)
    return result.reshape(members, levels, 1, pixels * region_count).astype(bf16)


def solution(mesh):
    return jax.shard_map(
        functools.partial(body, mesh.shape["region"], mesh.shape["lev"]),
        mesh=mesh,
        in_specs=(
            P(None, "lev", "region", None),
            P(None, "lev"),
            P(),
            P(),
            P(),
            P(),
            P(),
            P(),
            P(),
            P(),
        ),
        out_specs=P(None, "lev", "region", None),
        check_vma=False,
    )
```

```python
import functools

import jax
import jax.numpy as jnp
from jax import lax
from jax.experimental import pallas as pl
from jax.experimental.pallas import tpu as pltpu
from jax.sharding import PartitionSpec as P


TILE = 32
STRIDE = 4
LANES = 128
SUB = 8

highest = lax.Precision.HIGHEST
f32 = jnp.float32
bf16 = jnp.bfloat16


def dot(a, b, ca, cb, precision=highest):
    return lax.dot_general(
        a, b, (((ca,), (cb,)), ((), ())), precision=precision, preferred_element_type=f32
    )


def dot3(a, b, ca, cb):
    a_hi, b_hi = a.astype(bf16), b.astype(bf16)
    a_lo, b_lo = (a - a_hi.astype(f32)).astype(bf16), (b - b_hi.astype(f32)).astype(bf16)
    return dot(a_hi, b_hi, ca, cb, None) + (
        dot(a_hi, b_lo, ca, cb, None) + dot(a_lo, b_hi, ca, cb, None)
    )


def iota(shape, dim):
    return lax.broadcasted_iota(jnp.int32, shape, dim)


def split3(x):
    hi = x.astype(bf16)
    rest = x - hi.astype(f32)
    mid = rest.astype(bf16)
    low = (rest - mid.astype(f32)).astype(bf16)
    return hi, mid, low


def prior_kernel(first_ref, half_ref, *refs):
    inputs, (keep_ref, send_ref, aux_ref), held, arrived, grid_ref = (
        refs[:11], refs[11:14], refs[14:25], refs[25], refs[26]
    )
    copies = [
        pltpu.make_async_copy(source, target, arrived.at[i])
        for i, (source, target) in enumerate(zip(inputs, held))
    ]
    for copy in copies:
        copy.start()
    for copy in copies[:-1]:
        copy.wait()
    (down_ref, across_ref, home_ref, area_ref, radius_ref, height_ref, order_ref, place_ref, amount_ref, noise_ref,
     state_ref) = held
    members, levels, regions, pixels = state_ref.shape
    batches, size = order_ref.shape
    count = batches * size
    channels = height_ref.shape[1]
    sites = (TILE // STRIDE) * (TILE // STRIDE)

    lane = iota((1, count), 1)
    spread = jnp.where(
        iota((batches, count), 1) // size == iota((batches, count), 0), 1.0, 0.0
    ).astype(f32)
    order = jnp.concatenate([order_ref[k : k + 1] for k in range(batches)], axis=1)
    hit = order == iota((size, count), 0)
    rows = []
    for ref in (place_ref, amount_ref, noise_ref):
        if ref is place_ref and batches <= SUB and size <= LANES:
            square = jnp.concatenate([ref[...].astype(f32)] + [jnp.zeros((1, size), f32)] * (SUB - batches), axis=0)
            square = jnp.concatenate([square, jnp.zeros((SUB, LANES - size), f32)], axis=1)
            upright = square.T
            wide = jnp.zeros((size, count), f32)
            for k in range(batches):
                wide = jnp.where(lane // size == k, upright[:size, k : k + 1], wide)
        else:
            wide = dot(ref[...].astype(f32), spread, 0, 0)
        rows.append(jnp.sum(jnp.where(hit, wide, 0.0), axis=0, keepdims=True))
    picked = rows[0].astype(jnp.int32)
    channel = picked // sites
    cut = jnp.zeros((1, count), jnp.int32)
    for c in range(channels):
        cut = jnp.where(channel == c, radius_ref[c], cut)
    area = jnp.zeros((1, count), jnp.int32)
    for k in range(batches):
        area = jnp.where(lane // size == k, area_ref[k], area)
    rows += [cut.astype(f32), area.astype(f32), jnp.zeros((SUB - 5, count), f32)]
    aux_ref[...] = jnp.concatenate(rows, axis=0)
    spot = picked - channel * sites
    spot_row = spot // (TILE // STRIDE)
    spot_col = spot - spot_row * (TILE // STRIDE)
    heights = jnp.zeros((levels, count), f32)
    for c in range(channels):
        heights = jnp.where(channel == c, height_ref[:, c : c + 1], heights)

    pixel = iota((pixels, 1), 0) + first_ref[0]
    row = pixel // TILE
    col = pixel - row * TILE
    weight_row = jnp.zeros((pixels, 1), f32)
    weight_col = jnp.zeros((pixels, 1), f32)
    for i in range(STRIDE):
        weight_row = jnp.where(row % STRIDE == i, down_ref[i], weight_row)
        weight_col = jnp.where(col % STRIDE == i, across_ref[i], weight_col)
    weight = weight_row * weight_col
    inside = (row // STRIDE == spot_row) & (col // STRIDE == spot_col)
    place = jnp.where(inside, weight, 0.0)

    weights = [place * heights[level : level + 1] for level in range(levels)]
    copies[-1].wait()
    if pixels == LANES and LANES % size == 0 and count % LANES == 0:
        for level in range(levels):
            grid_ref[level] = state_ref[:, level].astype(f32).reshape(members * regions, pixels)
        together = LANES // size
        tiles = []
        for tile in range(count // LANES):
            heavy = jnp.concatenate(
                [w[:, LANES * tile : LANES * tile + LANES] for w in weights], axis=0
            )
            high = heavy.astype(bf16)
            low = (heavy - high.astype(f32)).astype(bf16)
            rows = []
            for k in range(tile * together, (tile + 1) * together):
                pick = pl.ds(home_ref[k], members, stride=regions)
                parts = [grid_ref[level, pick, :].astype(bf16) for level in range(levels)]
                rows.append(jnp.concatenate(parts, axis=1))
            grid = jnp.concatenate(rows, axis=0)
            value = dot(grid, high, 1, 0, None) + dot(grid, low, 1, 0, None)
            best = value[:members]
            for i in range(1, together):
                mine = iota((1, LANES), 1) // size == i
                best = jnp.where(mine, value[members * i : members * i + members], best)
            tiles.append(best)
        share = jnp.concatenate(tiles, axis=1)
    else:
        total = jnp.zeros((members * regions, count), f32)
        for level in range(levels):
            grid = state_ref[:, level].astype(f32).reshape(members * regions, pixels)
            for piece in split3(weights[level]):
                total = total + dot(grid.astype(bf16), piece, 1, 0, None)
        home = jnp.zeros((1, count), jnp.int32)
        for k in range(batches):
            home = jnp.where(lane // size == k, home_ref[k], home)
        here = iota((regions, count), 0) == home
        total = total.reshape(members, regions, count)
        share = jnp.sum(jnp.where(here[None], total, 0.0), axis=1)
    half = keep_ref.shape[0]
    if 2 * half > members:
        share = jnp.concatenate([share, jnp.zeros((2 * half - members, count), f32)], axis=0)
    first = half_ref[0] == 0
    keep_ref[...] = jnp.where(first, share[:half], share[half:])
    send_ref[...] = jnp.where(first, share[half:], share[:half])


def rep(x):
    return jnp.broadcast_to(x, (SUB, x.shape[1]))


def col(x, j):
    if x.shape[1] < LANES:
        x = jnp.concatenate([x, jnp.zeros((SUB, LANES - x.shape[1]), f32)], axis=1)
    return jnp.take_along_axis(x, jnp.full((SUB, LANES), j, jnp.int32), axis=1)


def filter_kernel(
    members, batches, own_ref, half_ref, mine_ref, other_ref, aux_ref, high_ref, low_ref,
    x_ref, h_ref, b_ref, row_ref, pair_ref,
):
    padded, count = 2 * mine_ref.shape[0], mine_ref.shape[1]
    size = count // batches
    groups = size // SUB
    dof = members - 1.0
    E = padded
    lane = iota((1, LANES), 1)
    member = lane < members

    first = half_ref[0] == 0
    mine, other = mine_ref[...], other_ref[...]
    base = jnp.concatenate(
        [jnp.where(first, mine, other), jnp.where(first, other, mine)], axis=0
    )
    if padded < LANES:
        base = jnp.concatenate([base, jnp.zeros((LANES - padded, count), f32)], axis=0)
    cols = base.T
    aux = aux_ref[...]
    aux_cols = jnp.concatenate([aux, jnp.zeros((LANES - SUB, count), f32)], axis=0).T
    center = jnp.sum(jnp.where(member, cols, 0.0), axis=1, keepdims=True) / members
    x_ref[:count] = jnp.where(
        lane == E, center - aux_cols[:, 1:2], jnp.where(member, cols - center, 0.0)
    )
    square = iota((LANES, LANES), 0)
    x_ref[count:] = jnp.where((square == iota((LANES, LANES), 1)) & (square < members), 1.0, 0.0)

    inverse_cut = 1.0 / (aux_cols[:, 3:4] + 1.0)
    noise = aux_cols[:, 2:3] * dof

    wide = count + LANES
    own = jnp.zeros((1, LANES), f32) + own_ref[0].astype(f32)
    owner = jnp.concatenate([aux[4:5], own], axis=1)

    for b in range(batches):
        r0 = b * size
        xb = x_ref[r0 : r0 + size]
        xm = jnp.where(member, xb, 0.0)
        gram = dot(xm, xm, 1, 1)
        noise_b = noise[r0 : r0 + size]
        gram = gram + jnp.where(iota((size, size), 0) == iota((size, size), 1), noise_b, 0.0)
        G = [gram[SUB * g : SUB * g + SUB] for g in range(groups)]
        X = [xb[SUB * g : SUB * g + SUB] for g in range(groups)]
        for p in range(groups):
            C = [[col(G[g], SUB * p + j) for g in range(p, groups)] for j in range(SUB)]
            s = [[rep(C[j][0][i : i + 1]) for j in range(i + 1)] for i in range(SUB)]
            noise_p = jnp.broadcast_to(noise_b[SUB * p : SUB * p + SUB], (SUB, LANES))
            l = [[None] * SUB for _ in range(SUB)]
            inv = []
            for j in range(SUB):
                inv.append(1.0 / s[j][j])
                for i in range(j + 1, SUB):
                    l[i][j] = s[i][j] * inv[j]
                for i in range(j + 1, SUB):
                    for k in range(j + 1, i + 1):
                        s[i][k] = s[i][k] - l[i][j] * s[k][j]
            U, alpha = [], []
            scaled = []
            pair_ref[:, :size] = G[p]
            pair_ref[:, LANES:] = X[p]
            for j in range(SUB):
                share = rep(noise_p[j : j + 1]) * inv[j]
                inv_alpha = 1.0 + share * lax.rsqrt(share)
                alpha.append(1.0 / inv_alpha)
                u = rep(pair_ref[j : j + 1, :size])
                h = rep(pair_ref[j : j + 1, LANES:])
                for i in range(j):
                    u = u - l[j][i][:, :size] * U[i]
                    h = h - l[j][i] * scaled[i]
                h = jnp.where(lane == E, h * inv_alpha, h)
                U.append(u)
                scaled.append(alpha[j] * h)
                row = jnp.where(lane == E + 1, alpha[j] * inv[j], h)
                h_ref[SUB * p + j : SUB * p + j + 1] = row[:1]
            for g in range(p + 1, groups):
                L = []
                for j in range(SUB):
                    c = C[j][g - p]
                    for i in range(j):
                        c = c - L[i] * s[j][i]
                    L.append(c * inv[j])
                for j in range(SUB):
                    G[g] = G[g] - L[j][:, :size] * U[j]
                    X[g] = X[g] - L[j] * scaled[j]

        low = min((r0 + size) // LANES * LANES, count)
        span = wide - low
        hb = h_ref[...]
        hm = jnp.where(member, hb, 0.0)
        overlap = dot3(hm, hm, 1, 1)
        xr = x_ref[low:]
        W = dot3(hm, xr, 1, 1)
        far = jnp.abs(owner[:, low:] - aux_cols[r0 : r0 + size, 4:5])
        taper = jnp.maximum(0.0, 1.0 - far * inverse_cut[r0 : r0 + size]) * hb[:, E + 1 : E + 2]
        S = [overlap[SUB * g : SUB * g + SUB] for g in range(groups)]
        W = [W[SUB * g : SUB * g + SUB] for g in range(groups)]
        tiles = span // LANES

        def scale(c, row):
            return jnp.concatenate(
                [c * row[:, LANES * t : LANES * t + LANES] for t in range(tiles)], axis=1
            )

        for p in range(groups):
            C = [[col(S[g], SUB * p + j) for g in range(p, groups)] for j in range(SUB)]
            B = []
            row_ref[:, : LANES * tiles] = W[p]
            for j in range(SUB):
                w = rep(row_ref[j : j + 1, : LANES * tiles])
                for i in range(j):
                    w = w - scale(rep(C[i][0][j : j + 1]), B[i])
                beta = w * rep(taper[SUB * p + j : SUB * p + j + 1])
                B.append(beta)
                b_ref[SUB * p + j : SUB * p + j + 1, low:] = beta[:1]
            for g in range(p + 1, groups):
                for j in range(SUB):
                    W[g] = W[g] - scale(C[j][g - p], B[j])
        x_ref[low:] = xr - dot3(b_ref[:, low:], hb, 0, 0)

    last = x_ref[count : count + members]
    mixing = jnp.where(member, last + last[:, E : E + 1], 0.0)
    mixing = mixing - jnp.sum(mixing, axis=0, keepdims=True) / members + 1.0 / members
    high = mixing.astype(bf16)
    high_ref[...] = high
    low_ref[...] = (mixing - high.astype(f32)).astype(bf16)


def apply_kernel(high_ref, low_ref, whole_ref, out_ref, row_ref, stage_ref, sent):
    sources, levels, members, pixels = whole_ref.shape
    high, low = high_ref[:, :members], low_ref[:, :members]
    parts = sent.shape[0]
    each = sources // parts
    copies = []
    for part in range(parts):
        group = range(part * each, part * each + each)
        for level in range(levels):
            field = jnp.concatenate([whole_ref[s, level] for s in group], axis=1)
            value = dot(high, field, 0, 0, None) + dot(low, field, 0, 0, None)
            for i, s in enumerate(group):
                piece = value[:, pixels * i : pixels * i + pixels]
                row_ref[s, pl.ds(level, members, stride=levels), :] = piece
        for s in group:
            piece = row_ref[s].reshape(members, levels, pixels).astype(bf16)
            stage_ref[:, :, pixels * s : pixels * s + pixels] = piece
        span = pl.ds(part * each * pixels, each * pixels)
        copies.append(
            pltpu.make_async_copy(stage_ref.at[:, :, span], out_ref.at[:, :, span], sent.at[part])
        )
        copies[-1].start()
    for copy in copies:
        copy.wait()


BOTH = ("region", "lev")


def swap(x, devices, k):
    return lax.ppermute(x, BOTH, [(i, i ^ k) for i in range(devices)])


def exchange(keep, send, state, devices):
    total = keep + swap(send, devices, 1)
    total, state = lax.optimization_barrier((total, state))
    state = jnp.transpose(state, (2, 1, 0, 3))
    stages = []
    bit = 8
    while bit < devices:
        stages.append((3 * bit, bit, 2 * bit) if 2 * bit < devices else (bit,))
        bit *= 4
    stages += [(k,) for k in (4, 2) if k < devices]
    for steps in stages:
        moved = [swap(total, devices, k) for k in steps]
        total = total + sum(moved)
    whole = lax.all_to_all(state, "region", split_axis=0, concat_axis=0, tiled=True)
    return total, swap(total, devices, 1), whole


def body(
    region_count,
    level_count,
    background_members,
    channel_height_kernel,
    sensor_spread_down,
    sensor_spread_across,
    measurement_placement,
    measurement_ordering,
    group_area_number,
    taper_radius_limit,
    measured_amounts,
    measurement_noise_spread,
):
    members, levels, pixels, regions = background_members.shape
    batches, size = measurement_ordering.shape
    count = batches * size
    own_region = lax.axis_index("region").astype(jnp.int32)

    state = jnp.transpose(background_members, (0, 1, 3, 2))
    if regions > 8:
        local = jnp.take(state, group_area_number, axis=2)
        home = jnp.arange(batches, dtype=jnp.int32)
    else:
        local, home = state, group_area_number
    half = -(-members // (2 * SUB)) * SUB
    devices = region_count * level_count
    side = ((own_region * level_count + lax.axis_index("lev")) % 2).astype(jnp.int32)[None]
    vmem = pl.BlockSpec(memory_space=pltpu.VMEM)
    smem = pl.BlockSpec(memory_space=pltpu.SMEM)
    scalars = (
        sensor_spread_down, sensor_spread_across, home, group_area_number, taper_radius_limit
    )
    tables = (
        jnp.transpose(channel_height_kernel),
        measurement_ordering,
        measurement_placement,
        measured_amounts,
        measurement_noise_spread,
        local,
    )
    keep, send, aux = pl.pallas_call(
        prior_kernel,
        out_shape=(
            jax.ShapeDtypeStruct((half, count), f32),
            jax.ShapeDtypeStruct((half, count), f32),
            jax.ShapeDtypeStruct((SUB, count), f32),
        ),
        in_specs=[smem] * 2 + [pl.BlockSpec(memory_space=pltpu.HBM)] * 11,
        out_specs=(vmem, vmem, vmem),
        scratch_shapes=[pltpu.SMEM(x.shape, x.dtype) for x in scalars]
        + [pltpu.VMEM(x.shape, x.dtype) for x in tables]
        + [
            pltpu.SemaphoreType.DMA((11,)),
            pltpu.VMEM((levels, members * local.shape[2], pixels), f32),
        ],
        compiler_params=pltpu.CompilerParams(vmem_limit_bytes=24 * 2**20),
    )(
        (own_region * pixels)[None],
        side,
        *[pltpu.with_memory_space_constraint(x, pltpu.HBM) for x in (*scalars, *tables)],
    )
    mine, other, whole = exchange(keep, send, state, devices)
    pieces = pl.pallas_call(
        functools.partial(filter_kernel, members, batches),
        out_shape=[jax.ShapeDtypeStruct((members, LANES), bf16)] * 2,
        in_specs=[smem] * 2 + [vmem] * 3,
        out_specs=[vmem, vmem],
        scratch_shapes=[
            pltpu.VMEM((count + LANES, LANES), f32),
            pltpu.VMEM((size, LANES), f32),
            pltpu.VMEM((size, count + LANES), f32),
            pltpu.VMEM((SUB, count + LANES), f32),
            pltpu.VMEM((SUB, 2 * LANES), f32),
        ],
        compiler_params=pltpu.CompilerParams(vmem_limit_bytes=16 * 2**20),
        cost_estimate=pl.CostEstimate(flops=10**9, bytes_accessed=10**6, transcendentals=0),
    )(own_region[None], side, mine, other, aux)

    if pixels % LANES == 0 and levels == 4:
        result = pl.pallas_call(
            apply_kernel,
            out_shape=jax.ShapeDtypeStruct((members, levels, pixels * region_count), bf16),
            in_specs=[vmem] * 3,
            out_specs=pl.BlockSpec(memory_space=pltpu.HBM),
            scratch_shapes=[
                pltpu.VMEM((region_count, members * levels, pixels), f32),
                pltpu.VMEM((members, levels, pixels * region_count), bf16),
                pltpu.SemaphoreType.DMA((4 if region_count % 4 == 0 else 1,)),
            ],
            compiler_params=pltpu.CompilerParams(vmem_limit_bytes=24 * 2**20),
        )(*pieces, whole)
        return result[:, :, None]
    field = jnp.transpose(whole, (2, 1, 0, 3)).reshape(members, -1)
    result = sum(dot(piece[:, :members], field, 0, 0, None) for piece in pieces)
    return result.reshape(members, levels, 1, pixels * region_count).astype(bf16)


def solution(mesh):
    return jax.shard_map(
        functools.partial(body, mesh.shape["region"], mesh.shape["lev"]),
        mesh=mesh,
        in_specs=(
            P(None, "lev", "region", None),
            P(None, "lev"),
            P(),
            P(),
            P(),
            P(),
            P(),
            P(),
            P(),
            P(),
        ),
        out_specs=P(None, "lev", "region", None),
        check_vma=False,
    )
```

```python
import functools

import jax
import jax.numpy as jnp
from jax import lax
from jax.experimental import pallas as pl
from jax.experimental.pallas import tpu as pltpu
from jax.sharding import PartitionSpec as P


TILE = 32
STRIDE = 4
LANES = 128
SUB = 8

highest = lax.Precision.HIGHEST
f32 = jnp.float32
bf16 = jnp.bfloat16


def dot(a, b, ca, cb, precision=highest):
    return lax.dot_general(
        a, b, (((ca,), (cb,)), ((), ())), precision=precision, preferred_element_type=f32
    )


def dot3(a, b, ca, cb):
    a_hi, b_hi = a.astype(bf16), b.astype(bf16)
    a_lo, b_lo = (a - a_hi.astype(f32)).astype(bf16), (b - b_hi.astype(f32)).astype(bf16)
    return dot(a_hi, b_hi, ca, cb, None) + (
        dot(a_hi, b_lo, ca, cb, None) + dot(a_lo, b_hi, ca, cb, None)
    )


def iota(shape, dim):
    return lax.broadcasted_iota(jnp.int32, shape, dim)


def split3(x):
    hi = x.astype(bf16)
    rest = x - hi.astype(f32)
    mid = rest.astype(bf16)
    low = (rest - mid.astype(f32)).astype(bf16)
    return hi, mid, low


def prior_kernel(first_ref, half_ref, *refs):
    inputs, (keep_ref, send_ref, aux_ref), held, arrived, grid_ref = (
        refs[:11], refs[11:14], refs[14:25], refs[25], refs[26]
    )
    copies = [
        pltpu.make_async_copy(source, target, arrived.at[i])
        for i, (source, target) in enumerate(zip(inputs, held))
    ]
    for copy in copies:
        copy.start()
    for copy in copies[:-1]:
        copy.wait()
    (down_ref, across_ref, home_ref, area_ref, radius_ref, height_ref, order_ref, place_ref, amount_ref, noise_ref,
     state_ref) = held
    members, levels, regions, pixels = state_ref.shape
    batches, size = order_ref.shape
    count = batches * size
    channels = height_ref.shape[1]
    sites = (TILE // STRIDE) * (TILE // STRIDE)

    lane = iota((1, count), 1)
    spread = jnp.where(
        iota((batches, count), 1) // size == iota((batches, count), 0), 1.0, 0.0
    ).astype(f32)
    order = jnp.concatenate([order_ref[k : k + 1] for k in range(batches)], axis=1)
    hit = order == iota((size, count), 0)
    rows = []
    for ref in (place_ref, amount_ref, noise_ref):
        wide = dot(ref[...].astype(f32), spread, 0, 0)
        rows.append(jnp.sum(jnp.where(hit, wide, 0.0), axis=0, keepdims=True))
    picked = rows[0].astype(jnp.int32)
    channel = picked // sites
    cut = jnp.zeros((1, count), jnp.int32)
    for c in range(channels):
        cut = jnp.where(channel == c, radius_ref[c], cut)
    area = jnp.zeros((1, count), jnp.int32)
    for k in range(batches):
        area = jnp.where(lane // size == k, area_ref[k], area)
    rows += [cut.astype(f32), area.astype(f32), jnp.zeros((SUB - 5, count), f32)]
    aux_ref[...] = jnp.concatenate(rows, axis=0)
    spot = picked - channel * sites
    spot_row = spot // (TILE // STRIDE)
    spot_col = spot - spot_row * (TILE // STRIDE)
    chosen = jnp.where(iota((channels, count), 0) == channel, 1.0, 0.0).astype(f32)
    heights = dot(height_ref[...], chosen, 1, 0)

    pixel = iota((pixels, 1), 0) + first_ref[0]
    row = pixel // TILE
    col = pixel - row * TILE
    weight_row = jnp.zeros((pixels, 1), f32)
    weight_col = jnp.zeros((pixels, 1), f32)
    for i in range(STRIDE):
        weight_row = jnp.where(row % STRIDE == i, down_ref[i], weight_row)
        weight_col = jnp.where(col % STRIDE == i, across_ref[i], weight_col)
    weight = weight_row * weight_col
    inside = (row // STRIDE == spot_row) & (col // STRIDE == spot_col)
    place = jnp.where(inside, weight, 0.0)

    weights = [place * heights[level : level + 1] for level in range(levels)]
    copies[-1].wait()
    if pixels == LANES and LANES % size == 0 and count % LANES == 0:
        for level in range(levels):
            grid = state_ref[:, level].astype(f32).reshape(members * regions, pixels)
            grid_ref[level, : members * regions] = grid
        together = LANES // size
        tiles = []
        for tile in range(count // LANES):
            heavy = jnp.concatenate(
                [w[:, LANES * tile : LANES * tile + LANES] for w in weights], axis=0
            )
            high = heavy.astype(bf16)
            low = (heavy - high.astype(f32)).astype(bf16)
            rows = []
            for k in range(tile * together, (tile + 1) * together):
                pick = pl.ds(home_ref[k], members, stride=regions)
                parts = [grid_ref[level, pick, :].astype(bf16) for level in range(levels)]
                rows.append(jnp.concatenate(parts, axis=1))
            grid = jnp.concatenate(rows, axis=0)
            value = dot(grid, high, 1, 0, None) + dot(grid, low, 1, 0, None)
            best = value[:members]
            for i in range(1, together):
                mine = iota((1, LANES), 1) // size == i
                best = jnp.where(mine, value[members * i : members * i + members], best)
            tiles.append(best)
        share = jnp.concatenate(tiles, axis=1)
    else:
        total = jnp.zeros((members * regions, count), f32)
        for level in range(levels):
            grid = state_ref[:, level].astype(f32).reshape(members * regions, pixels)
            for piece in split3(weights[level]):
                total = total + dot(grid.astype(bf16), piece, 1, 0, None)
        home = jnp.zeros((1, count), jnp.int32)
        for k in range(batches):
            home = jnp.where(lane // size == k, home_ref[k], home)
        here = iota((regions, count), 0) == home
        total = total.reshape(members, regions, count)
        share = jnp.sum(jnp.where(here[None], total, 0.0), axis=1)
    half = keep_ref.shape[0]
    if 2 * half > members:
        share = jnp.concatenate([share, jnp.zeros((2 * half - members, count), f32)], axis=0)
    first = half_ref[0] == 0
    keep_ref[...] = jnp.where(first, share[:half], share[half:])
    send_ref[...] = jnp.where(first, share[half:], share[:half])


def rep(x):
    return jnp.broadcast_to(x, (SUB, x.shape[1]))


def col(x, j):
    if x.shape[1] < LANES:
        x = jnp.concatenate([x, jnp.zeros((SUB, LANES - x.shape[1]), f32)], axis=1)
    return jnp.take_along_axis(x, jnp.full((SUB, LANES), j, jnp.int32), axis=1)


def filter_kernel(
    members, batches, own_ref, half_ref, mine_ref, other_ref, aux_ref, high_ref, low_ref,
    x_ref, h_ref, b_ref, row_ref, pair_ref,
):
    padded, count = 2 * mine_ref.shape[0], mine_ref.shape[1]
    size = count // batches
    groups = size // SUB
    dof = members - 1.0
    E = padded
    lane = iota((1, LANES), 1)
    member = lane < members

    first = half_ref[0] == 0
    mine, other = mine_ref[...], other_ref[...]
    base = jnp.concatenate(
        [jnp.where(first, mine, other), jnp.where(first, other, mine)], axis=0
    )
    if padded < LANES:
        base = jnp.concatenate([base, jnp.zeros((LANES - padded, count), f32)], axis=0)
    cols = base.T
    aux = aux_ref[...]
    aux_cols = jnp.concatenate([aux, jnp.zeros((LANES - SUB, count), f32)], axis=0).T
    center = jnp.sum(jnp.where(member, cols, 0.0), axis=1, keepdims=True) / members
    x_ref[:count] = jnp.where(
        lane == E, center - aux_cols[:, 1:2], jnp.where(member, cols - center, 0.0)
    )
    square = iota((LANES, LANES), 0)
    x_ref[count:] = jnp.where((square == iota((LANES, LANES), 1)) & (square < members), 1.0, 0.0)

    inverse_cut = 1.0 / (aux_cols[:, 3:4] + 1.0)
    noise = aux_cols[:, 2:3] * dof

    wide = count + LANES
    own = jnp.zeros((1, LANES), f32) + own_ref[0].astype(f32)
    owner = jnp.concatenate([aux[4:5], own], axis=1)

    for b in range(batches):
        r0 = b * size
        xb = x_ref[r0 : r0 + size]
        xm = jnp.where(member, xb, 0.0)
        gram = dot(xm, xm, 1, 1)
        noise_b = noise[r0 : r0 + size]
        gram = gram + jnp.where(iota((size, size), 0) == iota((size, size), 1), noise_b, 0.0)
        G = [gram[SUB * g : SUB * g + SUB] for g in range(groups)]
        X = [xb[SUB * g : SUB * g + SUB] for g in range(groups)]
        for p in range(groups):
            C = [[col(G[g], SUB * p + j) for g in range(p, groups)] for j in range(SUB)]
            s = [[rep(C[j][0][i : i + 1]) for j in range(i + 1)] for i in range(SUB)]
            noise_p = jnp.broadcast_to(noise_b[SUB * p : SUB * p + SUB], (SUB, LANES))
            l = [[None] * SUB for _ in range(SUB)]
            inv = []
            for j in range(SUB):
                inv.append(1.0 / s[j][j])
                for i in range(j + 1, SUB):
                    l[i][j] = s[i][j] * inv[j]
                for i in range(j + 1, SUB):
                    for k in range(j + 1, i + 1):
                        s[i][k] = s[i][k] - l[i][j] * s[k][j]
            U, alpha = [], []
            scaled = []
            pair_ref[:, :size] = G[p]
            pair_ref[:, LANES:] = X[p]
            for j in range(SUB):
                share = rep(noise_p[j : j + 1]) * inv[j]
                inv_alpha = 1.0 + share * lax.rsqrt(share)
                alpha.append(1.0 / inv_alpha)
                u = rep(pair_ref[j : j + 1, :size])
                h = rep(pair_ref[j : j + 1, LANES:])
                for i in range(j):
                    u = u - l[j][i][:, :size] * U[i]
                    h = h - l[j][i] * scaled[i]
                h = jnp.where(lane == E, h * inv_alpha, h)
                U.append(u)
                scaled.append(alpha[j] * h)
                row = jnp.where(lane == E + 1, alpha[j] * inv[j], h)
                h_ref[SUB * p + j : SUB * p + j + 1] = row[:1]
            for g in range(p + 1, groups):
                L = []
                for j in range(SUB):
                    c = C[j][g - p]
                    for i in range(j):
                        c = c - L[i] * s[j][i]
                    L.append(c * inv[j])
                for j in range(SUB):
                    G[g] = G[g] - L[j][:, :size] * U[j]
                    X[g] = X[g] - L[j] * scaled[j]

        low = min((r0 + size) // LANES * LANES, count)
        span = wide - low
        hb = h_ref[...]
        hm = jnp.where(member, hb, 0.0)
        overlap = dot3(hm, hm, 1, 1)
        xr = x_ref[low:]
        W = dot3(hm, xr, 1, 1)
        far = jnp.abs(owner[:, low:] - aux_cols[r0 : r0 + size, 4:5])
        taper = jnp.maximum(0.0, 1.0 - far * inverse_cut[r0 : r0 + size]) * hb[:, E + 1 : E + 2]
        S = [overlap[SUB * g : SUB * g + SUB] for g in range(groups)]
        W = [W[SUB * g : SUB * g + SUB] for g in range(groups)]
        tiles = span // LANES

        def scale(c, row):
            return jnp.concatenate(
                [c * row[:, LANES * t : LANES * t + LANES] for t in range(tiles)], axis=1
            )

        for p in range(groups):
            C = [[col(S[g], SUB * p + j) for g in range(p, groups)] for j in range(SUB)]
            B = []
            row_ref[:, : LANES * tiles] = W[p]
            for j in range(SUB):
                w = rep(row_ref[j : j + 1, : LANES * tiles])
                for i in range(j):
                    w = w - scale(rep(C[i][0][j : j + 1]), B[i])
                beta = w * rep(taper[SUB * p + j : SUB * p + j + 1])
                B.append(beta)
                b_ref[SUB * p + j : SUB * p + j + 1, low:] = beta[:1]
            for g in range(p + 1, groups):
                for j in range(SUB):
                    W[g] = W[g] - scale(C[j][g - p], B[j])
        x_ref[low:] = xr - dot3(b_ref[:, low:], hb, 0, 0)

    last = x_ref[count : count + members]
    mixing = jnp.where(member, last + last[:, E : E + 1], 0.0)
    mixing = mixing - jnp.sum(mixing, axis=0, keepdims=True) / members + 1.0 / members
    high = mixing.astype(bf16)
    high_ref[...] = high
    low_ref[...] = (mixing - high.astype(f32)).astype(bf16)


def apply_kernel(high_ref, low_ref, whole_ref, out_ref, row_ref, stage_ref, sent):
    sources, levels, members, pixels = whole_ref.shape
    high, low = high_ref[:, :members], low_ref[:, :members]
    parts = sent.shape[0]
    each = sources // parts
    copies = []
    for part in range(parts):
        group = range(part * each, part * each + each)
        for level in range(levels):
            field = jnp.concatenate([whole_ref[s, level] for s in group], axis=1)
            value = dot(high, field, 0, 0, None) + dot(low, field, 0, 0, None)
            for i, s in enumerate(group):
                piece = value[:, pixels * i : pixels * i + pixels]
                row_ref[s, pl.ds(level, members, stride=levels), :] = piece
        for s in group:
            piece = row_ref[s, : members * levels].reshape(members, levels, pixels).astype(bf16)
            stage_ref[:, :, pixels * s : pixels * s + pixels] = piece
        span = pl.ds(part * each * pixels, each * pixels)
        copies.append(
            pltpu.make_async_copy(stage_ref.at[:, :, span], out_ref.at[:, :, span], sent.at[part])
        )
        copies[-1].start()
    for copy in copies:
        copy.wait()


BOTH = ("region", "lev")


def swap(x, devices, k):
    return lax.ppermute(x, BOTH, [(i, i ^ k) for i in range(devices)])


def exchange(keep, send, state, devices):
    total = keep + swap(send, devices, 1)
    total, state = lax.optimization_barrier((total, state))
    state = jnp.transpose(state, (2, 1, 0, 3))
    stages = []
    bit = 8
    while bit < devices:
        stages.append((3 * bit, 2 * bit, bit) if 2 * bit < devices else (bit,))
        bit *= 4
    stages += [(k,) for k in (4, 2) if k < devices]
    for steps in stages:
        moved = [swap(total, devices, k) for k in steps]
        total = total + sum(moved)
    whole = lax.all_to_all(state, "region", split_axis=0, concat_axis=0, tiled=True)
    return total, swap(total, devices, 1), whole


def body(
    region_count,
    level_count,
    background_members,
    channel_height_kernel,
    sensor_spread_down,
    sensor_spread_across,
    measurement_placement,
    measurement_ordering,
    group_area_number,
    taper_radius_limit,
    measured_amounts,
    measurement_noise_spread,
):
    members, levels, pixels, regions = background_members.shape
    batches, size = measurement_ordering.shape
    count = batches * size
    own_region = lax.axis_index("region").astype(jnp.int32)

    state = jnp.transpose(background_members, (0, 1, 3, 2))
    if regions > 8:
        local = jnp.take(state, group_area_number, axis=2)
        home = jnp.arange(batches, dtype=jnp.int32)
    else:
        local, home = state, group_area_number
    half = -(-members // (2 * SUB)) * SUB
    devices = region_count * level_count
    side = ((own_region * level_count + lax.axis_index("lev")) % 2).astype(jnp.int32)[None]
    vmem = pl.BlockSpec(memory_space=pltpu.VMEM)
    smem = pl.BlockSpec(memory_space=pltpu.SMEM)
    scalars = (
        sensor_spread_down, sensor_spread_across, home, group_area_number, taper_radius_limit
    )
    tables = (
        jnp.transpose(channel_height_kernel),
        measurement_ordering,
        measurement_placement,
        measured_amounts,
        measurement_noise_spread,
        local,
    )
    keep, send, aux = pl.pallas_call(
        prior_kernel,
        out_shape=(
            jax.ShapeDtypeStruct((half, count), f32),
            jax.ShapeDtypeStruct((half, count), f32),
            jax.ShapeDtypeStruct((SUB, count), f32),
        ),
        in_specs=[smem] * 2 + [pl.BlockSpec(memory_space=pltpu.HBM)] * 11,
        out_specs=(vmem, vmem, vmem),
        scratch_shapes=[pltpu.SMEM(x.shape, x.dtype) for x in scalars]
        + [pltpu.VMEM(x.shape, x.dtype) for x in tables]
        + [
            pltpu.SemaphoreType.DMA((11,)),
            pltpu.VMEM((levels, (members + 1) * local.shape[2], pixels), f32),
        ],
        compiler_params=pltpu.CompilerParams(vmem_limit_bytes=24 * 2**20),
    )(
        (own_region * pixels)[None],
        side,
        *[pltpu.with_memory_space_constraint(x, pltpu.HBM) for x in (*scalars, *tables)],
    )
    mine, other, whole = exchange(keep, send, state, devices)
    pieces = pl.pallas_call(
        functools.partial(filter_kernel, members, batches),
        out_shape=[jax.ShapeDtypeStruct((members, LANES), bf16)] * 2,
        in_specs=[smem] * 2 + [vmem] * 3,
        out_specs=[vmem, vmem],
        scratch_shapes=[
            pltpu.VMEM((count + LANES, LANES), f32),
            pltpu.VMEM((size, LANES), f32),
            pltpu.VMEM((size, count + LANES), f32),
            pltpu.VMEM((SUB, count + LANES), f32),
            pltpu.VMEM((SUB, 2 * LANES), f32),
        ],
        compiler_params=pltpu.CompilerParams(vmem_limit_bytes=16 * 2**20),
        cost_estimate=pl.CostEstimate(flops=10**9, bytes_accessed=10**6, transcendentals=0),
    )(own_region[None], side, mine, other, aux)

    if pixels % LANES == 0 and levels == 4:
        result = pl.pallas_call(
            apply_kernel,
            out_shape=jax.ShapeDtypeStruct((members, levels, pixels * region_count), bf16),
            in_specs=[vmem] * 3,
            out_specs=pl.BlockSpec(memory_space=pltpu.HBM),
            scratch_shapes=[
                pltpu.VMEM((region_count, (members + 2) * levels, pixels), f32),
                pltpu.VMEM((members, levels, pixels * region_count), bf16),
                pltpu.SemaphoreType.DMA((2 if region_count % 2 == 0 else 1,)),
            ],
            compiler_params=pltpu.CompilerParams(vmem_limit_bytes=24 * 2**20),
        )(*pieces, whole)
        return result[:, :, None]
    field = jnp.transpose(whole, (2, 1, 0, 3)).reshape(members, -1)
    result = sum(dot(piece[:, :members], field, 0, 0, None) for piece in pieces)
    return result.reshape(members, levels, 1, pixels * region_count).astype(bf16)


def solution(mesh):
    return jax.shard_map(
        functools.partial(body, mesh.shape["region"], mesh.shape["lev"]),
        mesh=mesh,
        in_specs=(
            P(None, "lev", "region", None),
            P(None, "lev"),
            P(),
            P(),
            P(),
            P(),
            P(),
            P(),
            P(),
            P(),
        ),
        out_specs=P(None, "lev", "region", None),
        check_vma=False,
    )
```
